32 devices in a mesh: seq: 4 (over y, x), exp: 8 (over z, core).
Axes of the slice: x: 2, y: 2, z: 4, core: 2. Of those that a mesh axis runs over, the one named last changes fastest.
Arguments:
- inputs: bfloat16 [4096, 4096], P(('seq', 'exp')), may hold values from -6 to 6
- queries: bfloat16 [4096, 4096], P(('seq', 'exp')), may hold values from -40 to 40
- keys: bfloat16 [4096, 4096], P(('seq', 'exp')), may hold values from -4 to 4
- values: bfloat16 [4096, 4096], P(('seq', 'exp')), may hold values from -6 to 6
- norm_gain: float32 [4096], replicated, may hold values from 0.25 to 1.75
- expert_ids: int32 [4096, 2], P(('seq', 'exp')), may hold values from 0 to 7, all different within a row; in each aligned block of 128 rows (0 to 127, 128 to 255, ...) at most 32 rows name the same one
- gate_weights: float32 [4096, 2], P(('seq', 'exp')), may hold values from 0.2 to 1
- pairs: int32 [16, 2], replicated, may hold values from 0 to 7, as said below
- w_gate: bfloat16 [8, 4096, 4096], P('exp', None, 'seq'), may hold values from -0.09375 to 0.09375
- w_up: bfloat16 [8, 4096, 4096], P('exp', None, 'seq'), may hold values from -0.09375 to 0.09375
- w_down: bfloat16 [8, 4096, 4096], P('exp', 'seq'), may hold values from -0.09375 to 0.09375
Outputs:
- output: bfloat16 [4096, 4096], P(('seq', 'exp'))
The draws below stay inside these ranges and needn't reach their ends.
Inputs may be any that keep to these rules, and one draw needn't show every extreme that they name: `pairs`: each row is (query block, key block) with the key block from the query block - 2 to the query block; rows are distinct; every block is paired with itself; some pair has distance 2. `expert_ids`: the 2 ids of a token differ; within the 128 rows of one device every expert is named exactly 32 times.
All inputs are finite; a program needn't handle non-finite values.
Results may differ from the reference program's by a relative error of at most 0.007.
Values may be sent and summed in bfloat16 or wider, within the bound.
A program may use at most 128 MiB of HBM per device.

```python
import math
import jax
import jax.numpy as jnp
import numpy as np
from jax import lax

D = 4096
HEADS = 32
HSZ = 128
HD = 4096
FF = 4096
FFSLICE = 1024
EXPERTS = 8
TOP = 2
TOK_DEV = 128
TOKENS = 4096
CAP = 32
BLK = 512
DIST = 2
NBLK = 8
NEXTRA = 8
N_SEQ = 4


def drawn_fields(key):
    base_key = jax.random.fold_in(key, 7)
    key_first = jax.random.fold_in(base_key, 0)
    key_fourth = jax.random.fold_in(base_key, 3)
    key_field = jax.random.normal(key_first, (TOKENS, HD), jnp.float32)
    query_field = jax.random.normal(key_fourth, (TOKENS, HD), jnp.float32)
    return (jnp.clip(query_field, -40.0, 40.0), jnp.clip(key_field, -4.0, 4.0))


def draw_queries(key, part):
    return drawn_fields(key)[0].astype(jnp.bfloat16)


def draw_keys(key, part):
    return drawn_fields(key)[1].astype(jnp.bfloat16)


def draw_pairs(key, part):
    candidates = DIST * NBLK
    cand_index = jnp.arange(candidates, dtype=jnp.int32)
    query_block = cand_index // DIST
    distance = cand_index % DIST + 1
    priority = jax.random.permutation(jax.random.fold_in(key, 11), candidates).astype(jnp.int32)
    priority = jnp.where(query_block >= distance, priority, -1)
    priority = jnp.where((query_block == NBLK - 1) & (distance == DIST), candidates, priority)
    ignored, chosen = lax.top_k(priority, NEXTRA)
    extra_pairs = jnp.stack([query_block[chosen], query_block[chosen] - distance[chosen]], 1)
    block_ids = jnp.arange(NBLK, dtype=jnp.int32)
    diagonal = jnp.stack([block_ids, block_ids], 1)
    return jnp.concatenate([diagonal, extra_pairs], 0).astype(jnp.int32)


def steps_of(own_key, dims, cuts, low, top_value):
    factor_of = 1.0
    for dim, blocks in cuts:
        steps = jax.random.uniform(jax.random.fold_in(jax.random.fold_in(own_key, 6), dim), (blocks,), jnp.float32, low / len(cuts), top_value / len(cuts))
        factor_of = factor_of * jnp.repeat(jnp.exp(steps), dims[dim] // blocks).reshape((-1,) + (1,) * (len(dims) - 1 - dim))
    return factor_of


def deal_out(own_key, own, number, rows, count, top, reach, skew):
    sequence = jax.random.permutation(own_key, count)
    packed, common = shares(count, rows * top, reach, skew, True), shares(count, rows * top, reach, skew, False)
    places = jnp.arange(count)

    def named(sizes, rotation):
        used = int((sizes > 0).sum())
        fixed = max(1, used // 4)
        moved = fixed + (places - fixed + rotation * (used - fixed)) % max(1, count - fixed)
        return jnp.zeros((count,), jnp.int32).at[sequence[jnp.where(places < fixed, places, moved)]].set(jnp.asarray(sizes, jnp.int32))

    sizes = jnp.where(number % 4 == 0, named(packed, number // 4), named(common, number - number // 4 - 1))
    mixed = jax.random.permutation(jax.random.fold_in(own, 3), count)
    donor, taker = mixed[0:count // 2 * 2:2], mixed[1:count // 2 * 2:2]
    margin = jnp.minimum(sizes[donor] - 1, reach - sizes[taker]) // 2
    margin = jnp.where((donor == sequence[0]) | (taker == sequence[0]) | (sizes[taker] == 0), 0, jnp.maximum(margin, 0))
    moved = jax.random.randint(jax.random.fold_in(own, 4), (count // 2,), 0, 1 << 20) % (margin + 1)
    sizes = sizes.at[donor].add(-moved).at[taker].add(moved)
    members = jnp.searchsorted(jnp.cumsum(sizes), jnp.arange(rows * top), side="right").astype(jnp.int32)
    grid = members.reshape(top, rows).T
    grid = grid[jax.random.permutation(jax.random.fold_in(own, 1), rows)]
    rotation = jax.random.randint(jax.random.fold_in(own, 2), (rows, 1), 0, top)
    return jnp.take_along_axis(grid, (jnp.arange(top)[None, :] + rotation) % top, axis=1)


def shares(amount, total, bound, lean, full):
    portions = [(1 << 20) // math.isqrt(rank ** lean) + 1 for rank in range(1, amount + 1)]
    largest = bound if full else min(bound, max(-(-total // amount), total * portions[0] // sum(portions)))
    least = 1 if total - largest >= amount - 1 else 0
    counts, spare = [largest] + [least] * (amount - 1), total - largest - least * (amount - 1)
    while spare > 0:
        free = [i for i in range(1, amount) if counts[i] < largest] or [i for i in range(1, amount) if counts[i] < bound]
        mass, left = sum([portions[i] for i in free]), spare
        for i in free:
            more = min(bound - counts[i], max(1, left * portions[i] // mass), spare)
            counts[i] = counts[i] + more
            spare = spare - more
    return np.array(counts)


def gaussian(rng, extent, scale, reach, cuts=(), kind=jnp.bfloat16):
    gain = steps_of(rng, extent, cuts, -0.22, 0.18) if cuts else 1.0
    values = jax.random.normal(rng, extent, jnp.float32) * scale * gain
    return jnp.minimum(jnp.maximum(values, -reach), reach).astype(kind)


def setup_inputs(seed: int = 0) -> dict:
    key_list = jax.random.split(jax.random.key(seed), 12)
    inputs = gaussian(key_list[0], (TOKENS, D), 1.0, 6.0, ((0, 32),))
    queries = draw_queries(jax.random.fold_in(key_list[11], 71), 0)
    keys = draw_keys(jax.random.fold_in(key_list[11], 71), 0)
    values = gaussian(key_list[3], (TOKENS, HD), 1.0, 6.0, ((0, 32),))
    norm_gain = jnp.clip(1.0 + 0.15 * jax.random.normal(key_list[4], (D,), jnp.float32), 0.25, 1.75)
    expert_ids_keys = jax.random.split(jax.random.fold_in(key_list[5], 1), TOKENS // TOK_DEV)
    expert_ids_turns = jax.random.permutation(jax.random.fold_in(key_list[5], 3), TOKENS // TOK_DEV)
    expert_ids = jax.vmap(lambda own, number: deal_out(jax.random.fold_in(key_list[5], 2), own, number, TOK_DEV, EXPERTS, TOP, CAP, 2))(expert_ids_keys, expert_ids_turns).reshape((TOKENS, TOP))
    gate_weights = jnp.clip(jnp.exp(math.log(1.0) - 1.609438 * jax.random.uniform(key_list[6], (TOKENS, TOP), jnp.float32) ** steps_of(key_list[6], (TOKENS, TOP), ((0, 32),), -0.2, 0.2)), 0.2, 1.0)
    pairs = draw_pairs(jax.random.fold_in(key_list[11], 71), 0)
    w_gate = gaussian(key_list[8], (EXPERTS, D, FF), D ** -0.5, 0.09375, ((0, 8), (2, 4)))
    w_up = gaussian(key_list[9], (EXPERTS, D, FF), D ** -0.5, 0.09375, ((0, 8), (2, 4)))
    w_down = gaussian(key_list[10], (EXPERTS, FF, D), FF ** -0.5, 0.09375, ((0, 8), (1, 4)))
    return {"inputs": inputs, "queries": queries, "keys": keys, "values": values, "norm_gain": norm_gain, "expert_ids": expert_ids, "gate_weights": gate_weights, "pairs": pairs, "w_gate": w_gate, "w_up": w_up, "w_down": w_down}


very_negative = -1e+30
norm_epsilon = 1e-05

def reference(inputs, queries, keys, values, norm_gain, expert_ids, gate_weights, pairs, w_gate, w_up, w_down):
    score_scale = 1.0 / math.sqrt(HSZ)
    block_ids = jnp.arange(NBLK, dtype=jnp.int32)
    slot_ids = jnp.arange(DIST + 1, dtype=jnp.int32)
    wanted_key = block_ids[:, None] - (DIST - slot_ids)[None, :]
    present_table = jnp.any((pairs[None, None, :, 0] == block_ids[:, None, None]) & (pairs[None, None, :, 1] == wanted_key[:, :, None]), axis=2)
    zero_rows = jnp.zeros((DIST * BLK, HD), keys.dtype)
    keys_ext = jnp.concatenate([zero_rows, keys], 0)
    values_ext = jnp.concatenate([zero_rows, values], 0)

    def attend_block(block_index):
        query_rows = lax.dynamic_slice_in_dim(queries, block_index * BLK, BLK, 0).astype(jnp.float32).reshape(BLK, HEADS, HSZ)
        key_rows = lax.dynamic_slice_in_dim(keys_ext, block_index * BLK, (DIST + 1) * BLK, 0).astype(jnp.float32).reshape(-1, HEADS, HSZ)
        value_rows = lax.dynamic_slice_in_dim(values_ext, block_index * BLK, (DIST + 1) * BLK, 0).astype(jnp.float32).reshape(-1, HEADS, HSZ)
        scores = jnp.einsum('qhd,khd->hqk', query_rows, key_rows) * score_scale
        key_mask = jnp.repeat(present_table[block_index], BLK)
        scores = jnp.where(key_mask[None, None, :], scores, very_negative)
        row_top = lax.optimization_barrier(jnp.max(scores, axis=2, keepdims=True))
        exp_scores = jnp.exp(scores - row_top)
        denominator = lax.optimization_barrier(jnp.sum(exp_scores, axis=2))
        weights = lax.optimization_barrier(exp_scores.astype(jnp.bfloat16)).astype(jnp.float32)
        summed = jnp.einsum('hqk,khd->qhd', weights, value_rows)
        return (summed / jnp.transpose(denominator)[:, :, None]).astype(jnp.bfloat16).reshape(BLK, HD)
    attended = lax.map(attend_block, block_ids).reshape(TOKENS, HD)
    mixed_sum = inputs.astype(jnp.float32) + attended.astype(jnp.float32)
    mean_square = lax.optimization_barrier(jnp.mean(mixed_sum * mixed_sum, axis=1, keepdims=True))
    normed = (mixed_sum * lax.rsqrt(mean_square + norm_epsilon) * norm_gain[None, :]).astype(jnp.bfloat16)
    flat_ids = expert_ids.reshape(-1)
    per_expert = TOKENS * TOP // EXPERTS

    def serve(expert):
        chosen = jnp.argsort((flat_ids != expert).astype(jnp.int32), stable=True)[:per_expert].astype(jnp.int32)
        token_rows = normed[chosen // TOP]
        gate_value = jnp.dot(token_rows, w_gate[expert], preferred_element_type=jnp.float32)
        up_value = jnp.dot(token_rows, w_up[expert], preferred_element_type=jnp.float32)
        hidden = (jax.nn.silu(gate_value) * up_value).astype(jnp.bfloat16)
        running_sum = jnp.zeros((per_expert, D), jnp.float32)
        for run_index in range(N_SEQ):
            partial_value = jnp.dot(hidden[:, run_index * FFSLICE:(run_index + 1) * FFSLICE], w_down[expert, run_index * FFSLICE:(run_index + 1) * FFSLICE], preferred_element_type=jnp.float32)
            partial_value = lax.optimization_barrier(partial_value.astype(jnp.bfloat16))
            running_sum = running_sum + partial_value.astype(jnp.float32)
        return (chosen, running_sum)
    chosen_all, out_all = lax.map(serve, jnp.arange(EXPERTS, dtype=jnp.int32))
    contrib = jnp.zeros((TOKENS * TOP, D), jnp.float32).at[chosen_all.reshape(-1)].set(out_all.reshape(-1, D))
    contrib = contrib.reshape(TOKENS, TOP, D)
    output = mixed_sum + lax.optimization_barrier(jnp.sum(gate_weights[:, :, None] * contrib, axis=1))
    return output.astype(jnp.bfloat16)
```

```python
import functools
import math

import jax
import jax.numpy as jnp
from jax import lax
from jax.experimental import pallas as pl
from jax.experimental.pallas import tpu as pltpu
from jax.sharding import PartitionSpec as P

HSZ = 128
TOP = 2
BLK = 512
DIST = 2
OUTER = 2
CORES = 2

very_negative = -1e30
norm_epsilon = 1e-05

MESH = pl.DeviceIdType.MESH
ANY = pl.BlockSpec(memory_space=pl.ANY)
HELD = pl.BlockSpec(memory_space=pltpu.VMEM)
DMA = pltpu.SemaphoreType.DMA


def remote(source, target, send_sem, recv_sem, device):
    return pltpu.make_async_remote_copy(
        src_ref=source,
        dst_ref=target,
        send_sem=send_sem,
        recv_sem=recv_sem,
        device_id=device,
        device_id_type=MESH,
    )


def turned(index, steps, count):
    return lax.rem(index + (steps % count), count)


def xor(one, two, count):
    total, bit = 0, 1
    while bit < count:
        total = total + bit * lax.rem(lax.div(one, bit) + lax.div(two, bit), 2)
        bit *= 2
    return total


def loop(begin, end, body):
    def step(i, carry):
        body(i)
        return carry

    lax.fori_loop(begin, end, step, 0)


def wide(value):
    return value.astype(jnp.float32)


def layer_kernel(
    seq_count, exp_count, tail, together, tile, wide_tile, norm_tile,
    pairs_ref, ids_ref, gate_weight_ref, gain_ref, in_hbm, q_hbm, k_hbm, v_hbm, gate_hbm, up_hbm, down_hbm,
    out_ref,
    present, x_in, q_run, k_run, v_run, attended, outgoing, got, choose_ref, coarse_ref, fine_ref,
    gate_ref, up_ref, down_ref, buf, x_ref, hid_ref, in0, in1, out0, out1, mid0, mid1, done,
    in_sem, own_sem, q_send, q_recv, f_send, f_recv, a_own, a_send, a_recv,
    local_sem, stay_sem, w_sem, z_send, z_recv, x_send, x_recv, d_send, d_recv,
    p_send, p_recv, m_send, m_recv, g_send, g_recv,
):
    s, e = lax.axis_index("seq"), lax.axis_index("exp")
    z, c = lax.div(e, CORES), lax.rem(e, CORES)
    chips = exp_count // CORES
    rows, width = x_in.shape
    run, group = q_run.shape
    heads, blocks, owners = group // HSZ, run // BLK, BLK // rows
    slots = DIST + 1
    capacity = buf.shape[3]
    inner_count = seq_count // OUTER
    half = width // 2
    a, b = lax.div(s, inner_count), lax.rem(s, inner_count)
    other = 1 - a
    outer = (other * inner_count + b, e)
    steps = range(1, inner_count)
    forth = [turned(b, j, inner_count) for j in steps]
    back = [turned(b, -j, inner_count) for j in steps]
    inner = [(a * inner_count + f, e) for f in forth]
    low, high = pl.ds(0, half), pl.ds(half, half)
    groups = exp_count // together
    chunk_rows = seq_count * capacity

    def arrived(block, send_sem, recv_sem):
        remote(block, block, send_sem, recv_sem, (s, e)).wait_recv()

    def columns(ref, index):
        return ref.at[:, pl.ds(pl.multiple_of(index * group, group), group)]

    def place(index):
        return lax.rem(index, CORES) * chips + lax.div(index, CORES)

    def lines(ref, offset, index):
        return ref.at[pl.ds(pl.multiple_of(offset + index * rows, rows), rows)]

    def landing(i, owner):
        if i == 2:
            return lines(q_run, 0, place(owner))
        return lines((k_run, v_run)[i], tail, owner)

    sources = (k_hbm, v_hbm, q_hbm)

    def give(i, k):
        d = xor(e, k, exp_count)
        return remote(columns(sources[i], d), landing(i, e), q_send.at[i, k], q_recv.at[i, k], (s, d))

    def keep(i):
        return pltpu.make_async_copy(columns(sources[i], e), landing(i, e), own_sem.at[i])

    def taken(i, k):
        block = landing(i, xor(e, k, exp_count))
        arrived(block, q_send.at[i, k], q_recv.at[i, k])

    def relay(i, k, act):
        owner = xor(e, k, exp_count)
        inside = (owner + 1) * rows > run - tail
        row = pl.multiple_of(lax.max(owner * rows - (run - tail), 0), rows)
        copy = remote(
            landing(i, owner), (k_run, v_run)[i].at[pl.ds(row, rows)], f_send.at[i, k], f_recv.at[i, k],
            (turned(s, 1, seq_count), e),
        )
        if act == "start":
            pl.when(inside & (s < seq_count - 1))(copy.start)
        elif act == "send":
            pl.when(inside & (s < seq_count - 1))(copy.wait_send)
        else:
            pl.when(inside & (s > 0))(copy.wait_recv)

    barrier = pltpu.get_barrier_semaphore()
    for k in range(1, exp_count):
        pl.semaphore_signal(barrier, inc=1, device_id=(s, turned(e, k, exp_count)), device_id_type=MESH)
    for k in range(1, seq_count):
        pl.semaphore_signal(barrier, inc=1, device_id=(turned(s, k, seq_count), e), device_id_type=MESH)
    pl.semaphore_wait(barrier, exp_count + seq_count - 2)

    for i in range(2):
        for k in range(1, exp_count):
            give(i, k).start()

    @pl.when(c == 0)
    def _():
        for k in range(1, exp_count):
            give(2, k).start()

    for i in range(3):
        keep(i).start()
    inputs_copy = pltpu.make_async_copy(in_hbm, x_in, in_sem)
    inputs_copy.start()
    weights = [
        pltpu.make_async_copy(source.at[0], target, w_sem.at[i])
        for i, (source, target) in enumerate(
            ((gate_hbm, gate_ref), (up_hbm, up_ref), (down_hbm, down_ref))
        )
    ]
    for copy in weights:
        copy.start()

    first_block = s * blocks
    wanted = [(first_block + i, first_block + i - (DIST - j)) for i in range(blocks) for j in range(slots)]

    def seen(p, found):
        query, key = pairs_ref[p, 0], pairs_ref[p, 1]
        return tuple(
            f + jnp.where((query == w[0]) & (key == w[1]), 1, 0) for f, w in zip(found, wanted)
        )

    found = lax.fori_loop(0, pairs_ref.shape[0], seen, (jnp.int32(0),) * len(wanted))
    for i in range(blocks):
        for j in range(slots):
            present[i, j] = found[i * slots + j]

    places = exp_count * capacity
    named = [ids_ref[:, t : t + 1] for t in range(TOP)]
    ranks = lax.broadcasted_iota(jnp.int32, (rows, HSZ), 1)
    marks = [jnp.where(n == ranks, 1.0, 0.0) for n in named]
    earlier = jnp.where(
        lax.broadcasted_iota(jnp.int32, (rows, rows), 1) < lax.broadcasted_iota(jnp.int32, (rows, rows), 0),
        1.0, 0.0,
    ).astype(jnp.bfloat16)
    ahead = jnp.dot(earlier, sum(marks).astype(jnp.bfloat16), preferred_element_type=jnp.float32)
    slot_ids = lax.broadcasted_iota(jnp.int32, (rows, places), 1)
    choose = jnp.zeros((rows, places), jnp.float32)
    weight = jnp.zeros((rows, places), jnp.float32)
    for t in range(TOP):
        position = jnp.sum(ahead * marks[t], axis=1, keepdims=True)
        spot = named[t] * capacity + position.astype(jnp.int32) == slot_ids
        choose = jnp.where(spot, 1.0, choose)
        weight = jnp.where(spot, gate_weight_ref[:, t : t + 1], weight)
    choose_ref[...] = choose.astype(jnp.bfloat16)
    coarse = weight.astype(jnp.bfloat16)
    coarse_ref[...] = coarse
    fine_ref[...] = (weight - coarse.astype(jnp.float32)).astype(jnp.bfloat16)

    for i in range(2):
        keep(i).wait()
        relay(i, 0, "start")
        for k in range(1, exp_count):
            taken(i, k)
            relay(i, k, "start")
    keep(2).wait()

    def queries_of(parity):
        for j in range(chips):
            k = CORES * j + lax.rem(c + parity, CORES)
            if j == 0:
                pl.when(k > 0)(functools.partial(taken, 2, k))
            else:
                taken(2, k)

    queries_of(0)

    @pl.when(c > 0)
    def _():
        for k in range(1, exp_count):
            give(2, k).start()

    for i in range(2):
        for k in range(exp_count):
            relay(i, k, "recv")

    scale = 1.0 / math.sqrt(HSZ)

    def piece(owner, head):
        return q_run.at[
            pl.ds(pl.multiple_of(place(owner) * rows, rows), rows), pl.ds(pl.multiple_of(head * HSZ, HSZ), HSZ)
        ]

    def goal(giver, head):
        return attended.at[:, pl.ds(pl.multiple_of(giver * group + head * HSZ, HSZ), HSZ)]

    def send(owner, head):
        return remote(
            piece(owner, head), goal(e, head), a_send.at[owner, head], a_recv.at[e, head], (s, owner)
        )

    def own(head):
        return pltpu.make_async_copy(piece(e, head), goal(e, head), a_own.at[head])

    part = BLK // CORES

    def attend(parity):
        def step(i):
            head = lax.rem(i, heads)
            block = lax.rem(lax.div(e, owners) + 1 + lax.div(i, heads), blocks)
            column = pl.ds(pl.multiple_of(head * HSZ, HSZ), HSZ)
            mine = pl.ds(pl.multiple_of(parity * (run // CORES) + block * part, part), part)

            def span(slot):
                return pl.ds(pl.multiple_of((block + slot) * BLK, BLK), BLK)

            q = q_run[mine, column]
            scores = []
            for j in range(slots):
                score = lax.dot_general(
                    q, k_run[span(j), column], (((1,), (1,)), ((), ())), preferred_element_type=jnp.float32
                )
                scores.append(jnp.where(present[block, j] > 0, score * scale, very_negative))
            top = functools.reduce(jnp.maximum, [jnp.max(x, axis=1, keepdims=True) for x in scores])
            total, summed = 0.0, 0.0
            for j in range(slots):
                exps = jnp.exp(scores[j] - top)
                total = total + jnp.sum(exps, axis=1, keepdims=True)
                value = v_run[span(j), column]
                value = jnp.where(present[block, j] > 0, value, jnp.zeros_like(value))
                summed = summed + jnp.dot(
                    exps.astype(jnp.bfloat16), value, preferred_element_type=jnp.float32
                )
            q_run[mine, column] = (summed / total).astype(q_run.dtype)
            for j in range(owners // CORES):
                owner = block * owners + CORES * j + parity

                @pl.when(owner != e)
                def _():
                    send(owner, head).start()

                @pl.when(owner == e)
                def _():
                    own(head).start()

        loop(0, blocks * heads, step)

    def mixed(where):
        return wide(x_in[:, where]) + wide(attended[:, where])

    def chunk(t):
        return CORES * xor(z, lax.rem(t, chips), chips) + lax.div(t, chips)

    def spread(k):
        d = xor(e, k, exp_count)
        step = c * chips + lax.div(k, CORES)
        return remote(outgoing.at[d], buf.at[a, b, e], z_send.at[k], z_recv.at[step], (s, d))

    def stays():
        return pltpu.make_async_copy(outgoing.at[e], buf.at[a, b, e], local_sem)

    def dispatch():
        inputs_copy.wait()

        def squares(k, total):
            giver = xor(e, k, exp_count)

            @pl.when(k > 0)
            def _():
                for head in range(heads):
                    block = goal(giver, head)
                    arrived(block, a_send.at[giver, head], a_recv.at[giver, head])

            @pl.when(k == 0)
            def _():
                for head in range(heads):
                    own(head).wait()

            value = mixed(pl.ds(pl.multiple_of(giver * group, group), group))
            return total + jnp.sum(value * value, axis=1, keepdims=True)

        total = lax.fori_loop(0, exp_count, squares, jnp.zeros((rows, 1), jnp.float32))
        factor = lax.rsqrt(total / width + norm_epsilon)

        def normed_tile(n):
            where = pl.ds(pl.multiple_of(n * norm_tile, norm_tile), norm_tile)
            normed = (mixed(where) * factor * gain_ref[:, where]).astype(jnp.bfloat16)
            picked = lax.dot_general(
                choose_ref[...], normed, (((0,), (0,)), ((), ())), preferred_element_type=jnp.float32
            )
            outgoing[:, :, where] = picked.astype(outgoing.dtype).reshape(exp_count, capacity, norm_tile)

        loop(0, width // norm_tile, normed_tile)
        stays().start()
        loop(1, exp_count, lambda k: spread(k).start())

    attend(0)
    pl.when(c == 0)(dispatch)
    queries_of(1)
    attend(1)
    pl.when(c > 0)(dispatch)

    def directs(k):
        block = buf.at[a, b, chunk(k)]
        return [
            remote(block, block, x_send.at[i, k], x_recv.at[i, k], peer)
            for i, peer in enumerate([outer] + inner)
        ]

    def relays(k):
        n = chunk(k)
        copies = []
        for j, peer in enumerate(inner):
            block = buf.at[other, b, n, :, low]
            copies.append(remote(block, block, d_send.at[0, j, k], d_recv.at[0, j, k], peer))
            block = buf.at[a, back[j], n, :, high]
            copies.append(remote(block, block, d_send.at[1, j, k], d_recv.at[1, j, k], outer))
        return copies

    def gather_step(k):
        @pl.when(k < exp_count)
        def _():
            @pl.when(k != c * chips)
            def _():
                arrived(buf.at[a, b, chunk(k)], z_send.at[k], z_recv.at[k])

            @pl.when(k == c * chips)
            def _():
                stays().wait()

            for copy in directs(k):
                copy.start()

        @pl.when((k > 0) & (k <= exp_count))
        def _():
            n = k - 1
            m = chunk(n)
            arrived(buf.at[other, b, m], x_send.at[0, n], x_recv.at[0, n])
            for j in range(inner_count - 1):
                arrived(buf.at[a, back[j], m], x_send.at[1 + j, n], x_recv.at[1 + j, n])
            for copy in relays(n):
                copy.start()

    def complete(k):
        n = chunk(k)
        for j in range(inner_count - 1):
            for h, side in enumerate((low, high)):
                arrived(buf.at[other, back[j], n, :, side], d_send.at[h, j, k], d_recv.at[h, j, k])

    def first(k):
        n = chunk(k)
        return [
            remote(buf.at[other, :, n, :, high], in1.at[k], p_send.at[0, k], p_recv.at[0, k], outer)
        ] + [
            remote(
                buf.at[:, f, n, :, low], in0.at[j, k], p_send.at[1 + j, k], p_recv.at[1 + j, k], inner[j]
            )
            for j, f in enumerate(forth)
        ]

    def second(k):
        return [remote(out0.at[k], mid0.at[k], m_send.at[0, k], m_recv.at[0, k], outer)] + [
            remote(out1.at[j, k], mid1.at[j, k], m_send.at[1 + j, k], m_recv.at[1 + j, k], inner[j])
            for j in range(inner_count - 1)
        ]

    def third(k):
        d = chunk(k)
        where = xor(e, d, exp_count)
        return remote(done.at[k], got.at[e], g_send.at[k], g_recv.at[where], (s, d))

    def stay():
        return pltpu.make_async_copy(done.at[c * chips], got.at[e], stay_sem)

    def inner_sum(k, side):
        total = wide(buf[side, b, chunk(k), :, low])
        for j in range(inner_count - 1):
            total = total + wide(in0[j, k, side])
        return total

    def outer_sum(k, lane):
        return wide(buf[a, lane, chunk(k), :, high]) + wide(in1[k, lane])

    def sum_step(k):
        @pl.when((k >= 0) & (k < exp_count))
        def _():
            sends = second(k)
            for j in range(inner_count - 1):
                arrived(in0.at[j, k], p_send.at[1 + j, k], p_recv.at[1 + j, k])
            out0[k] = inner_sum(k, other).astype(out0.dtype)
            sends[0].start()
            arrived(in1.at[k], p_send.at[0, k], p_recv.at[0, k])
            for j, f in enumerate(forth):
                out1[j, k] = outer_sum(k, f).astype(out1.dtype)
                sends[1 + j].start()

        @pl.when((k > 0) & (k <= exp_count))
        def _():
            n = k - 1
            arrived(mid0.at[n], m_send.at[0, n], m_recv.at[0, n])
            done[n, :, low] = (inner_sum(n, a) + wide(mid0[n])).astype(done.dtype)
            total = outer_sum(n, b)
            for j in range(inner_count - 1):
                arrived(mid1.at[j, n], m_send.at[1 + j, n], m_recv.at[1 + j, n])
                total = total + wide(mid1[j, n])
            done[n, :, high] = total.astype(done.dtype)

            @pl.when(n == c * chips)
            def _():
                stay().start()

            @pl.when(n != c * chips)
            def _():
                third(n).start()

    loop(0, together + 2, gather_step)
    for copy in weights:
        copy.wait()
    tiles, wide_tiles = hid_ref.shape[1] // tile, width // wide_tile
    stride, wide_stride = max(1, tiles // together), max(1, wide_tiles // together)

    def expert_group(p):
        base = p * together
        for i in range(together):
            complete(base + i)
            x_ref[pl.ds(i * chunk_rows, chunk_rows)] = buf[:, :, chunk(base + i)].reshape(chunk_rows, width)

        def hidden_tile(n):
            where = pl.ds(pl.multiple_of(n * tile, tile), tile)
            x = x_ref[...]
            gate = jnp.dot(x, gate_ref[:, where], preferred_element_type=jnp.float32)
            up = jnp.dot(x, up_ref[:, where], preferred_element_type=jnp.float32)
            hid_ref[:, where] = (jax.nn.silu(gate) * up).astype(hid_ref.dtype)

            @pl.when(lax.rem(n, stride) == 0)
            def _():
                gather_step(base + together + 2 + lax.div(n, stride))

        loop(0, tiles, hidden_tile)
        for i in range(together):
            for copy in directs(base + i) + relays(base + i):
                copy.wait_send()

        def down_tile(n):
            where = pl.ds(pl.multiple_of(n * wide_tile, wide_tile), wide_tile)
            y = jnp.dot(hid_ref[...], down_ref[:, where], preferred_element_type=jnp.float32).astype(buf.dtype)
            for i in range(together):
                buf[:, :, chunk(base + i), :, where] = y[i * chunk_rows : (i + 1) * chunk_rows].reshape(
                    OUTER, inner_count, capacity, wide_tile
                )

            @pl.when(lax.rem(n, wide_stride) == 0)
            def _():
                sum_step(base - together + lax.div(n, wide_stride))

        loop(0, wide_tiles, down_tile)
        for i in range(together):
            for copy in first(base + i):
                copy.start()

    loop(0, groups, expert_group)
    loop((groups - 1) * together, exp_count + 1, sum_step)

    stay().wait()
    for k in range(1, exp_count):
        arrived(got.at[xor(e, k, exp_count)], g_send.at[k], g_recv.at[k])

    def final_tile(n):
        where = pl.ds(pl.multiple_of(n * norm_tile, norm_tile), norm_tile)
        flat = got[:, :, where].reshape(places, norm_tile)
        combined = jnp.dot(coarse_ref[...], flat, preferred_element_type=jnp.float32) + jnp.dot(
            fine_ref[...], flat, preferred_element_type=jnp.float32
        )
        out_ref[:, where] = (mixed(where) + combined).astype(out_ref.dtype)

    loop(0, width // norm_tile, final_tile)

    for i in range(2):
        for k in range(exp_count):
            relay(i, k, "send")
    for i in range(3):
        for k in range(1, exp_count):
            give(i, k).wait_send()

    def finish(k):
        for copy in first(k) + second(k):
            copy.wait_send()

        @pl.when(k > 0)
        def _():
            spread(k).wait_send()
            for head in range(heads):
                send(xor(e, k, exp_count), head).wait_send()

        @pl.when(k != c * chips)
        def _():
            third(k).wait_send()

    loop(0, exp_count, finish)


def per_device(
    inputs, queries, keys, values, norm_gain, expert_ids, gate_weights, pairs, w_gate, w_up, w_down
):
    rows, width = inputs.shape
    seq_count, exp_count = lax.axis_size("seq"), lax.axis_size("exp")
    tail = DIST * BLK
    run, group = rows * exp_count, queries.shape[1] // exp_count
    heads, blocks = group // HSZ, run // BLK
    capacity = rows * TOP // exp_count
    places = exp_count * capacity
    hidden = w_gate.shape[2]
    inner_count = seq_count // OUTER
    inner_peers = inner_count - 1
    half = width // 2
    kind = inputs.dtype
    together = 1
    while 2 * together * seq_count * capacity <= 256 and exp_count % (2 * together) == 0:
        together *= 2
    group_rows = together * seq_count * capacity
    tile, wide_tile, norm_tile = min(256, hidden // together), min(512, width // together), min(512, width)
    vmem = [
        (rows, width),
        (run, group),
        (tail + run, group),
        (tail + run, group),
        (rows, width),
        (exp_count, capacity, width),
        (exp_count, capacity, width),
        (rows, places),
        (rows, places),
        (rows, places),
        w_gate.shape[1:],
        w_up.shape[1:],
        w_down.shape[1:],
        (OUTER, inner_count, exp_count, capacity, width),
        (group_rows, width),
        (group_rows, hidden),
        (inner_peers, exp_count, OUTER, capacity, half),
        (exp_count, inner_count, capacity, half),
        (exp_count, capacity, half),
        (inner_peers, exp_count, capacity, half),
        (exp_count, capacity, half),
        (inner_peers, exp_count, capacity, half),
        (exp_count, capacity, width),
    ]
    one, per_peer, per_side = (exp_count,), (inner_count, exp_count), (2, inner_peers, exp_count)
    sems = [
        (3, exp_count), (3, exp_count), (2, exp_count), (2, exp_count), (heads,), (exp_count, heads),
        (exp_count, heads),
    ]
    more = [one, one, per_peer, per_peer, per_side, per_side, per_peer, per_peer, per_peer, per_peer, one, one]
    return pl.pallas_call(
        functools.partial(layer_kernel, seq_count, exp_count, tail, together, tile, wide_tile, norm_tile),
        out_shape=jax.ShapeDtypeStruct((rows, width), kind),
        in_specs=[pl.BlockSpec(memory_space=pltpu.SMEM)] + [HELD] * 3 + [ANY] * 7,
        out_specs=HELD,
        scratch_shapes=[pltpu.SMEM((blocks, DIST + 1), jnp.int32)]
        + [pltpu.VMEM(shape, kind) for shape in vmem]
        + [DMA, DMA((3,))]
        + [DMA(shape) for shape in sems]
        + [DMA, DMA, DMA((3,))]
        + [DMA(shape) for shape in more],
        compiler_params=pltpu.CompilerParams(
            collective_id=1, has_side_effects=True, vmem_limit_bytes=67043328
        ),
        name="layer",
    )(
        pairs, expert_ids, gate_weights, norm_gain.reshape(1, width), inputs, queries, keys, values,
        w_gate, w_up, w_down,
    )


def solution(mesh):
    rows = P(("seq", "exp"), None)
    in_specs = (
        rows, rows, rows, rows, P(), rows, rows, P(),
        P("exp", None, "seq"), P("exp", None, "seq"), P("exp", "seq", None),
    )
    return jax.shard_map(
        per_device, mesh=mesh, in_specs=in_specs, out_specs=rows, check_vma=False
    )
```

```python
import functools
import math

import jax
import jax.numpy as jnp
from jax import lax
from jax.experimental import pallas as pl
from jax.experimental.pallas import tpu as pltpu
from jax.sharding import PartitionSpec as P

HSZ = 128
TOP = 2
BLK = 512
DIST = 2
OUTER = 2
CORES = 2
PARTS = 4

very_negative = -1e30
norm_epsilon = 1e-05

MESH = pl.DeviceIdType.MESH
ANY = pl.BlockSpec(memory_space=pl.ANY)
HELD = pl.BlockSpec(memory_space=pltpu.VMEM)
DMA = pltpu.SemaphoreType.DMA


def remote(source, target, send_sem, recv_sem, device):
    return pltpu.make_async_remote_copy(
        src_ref=source,
        dst_ref=target,
        send_sem=send_sem,
        recv_sem=recv_sem,
        device_id=device,
        device_id_type=MESH,
    )


def turned(index, steps, count):
    return lax.rem(index + (steps % count), count)


def xor(one, two, count):
    total, bit = 0, 1
    while bit < count:
        total = total + bit * lax.rem(lax.div(one, bit) + lax.div(two, bit), 2)
        bit *= 2
    return total


def loop(begin, end, body):
    def step(i, carry):
        body(i)
        return carry

    lax.fori_loop(begin, end, step, 0)


def wide(value):
    return value.astype(jnp.float32)


EIGHT_ORDER = ((0, 0), (2, 0), (1, 0), (3, 0), (3, 1), (1, 1), (2, 1), (0, 1))
EIGHT_STEPS = (
    ("V", 0), ("q", 0), ("a", (0, 0)), ("a", (0, 1)), ("a", (0, 2)), ("a", (0, 3)), ("m", 0), ("t", 0), ("q",
    1), ("x", (0, 4)), ("x", (0, 5)), ("x", (0, 2)), ("x", (0, 3)), ("x", (0, 6)), ("x", (0, 1)), ("a", (1,
    0)), ("a", (1, 1)), ("x", (0, 7)), ("a", (1, 2)), ("g", 0), ("g", 1), ("r", 0), ("a", (1, 3)), ("r", 1),
    ("g", 2), ("m", 1), ("x", (1, 2)), ("g", 3), ("c", 0), ("h", (0, 0)), ("h", (0, 1)), ("x", (1, 3)), ("r",
    2), ("h", (0, 2)), ("h", (0, 3)), ("x", (1, 1)), ("r", 3), ("x", (1, 7)), ("s", 0), ("x", (1, 6)), ("d",
    (0, 0)), ("d", (0, 1)), ("f", 0), ("f", 1), ("c", 1), ("A", 0), ("x", (1, 4)), ("h", (1, 0)), ("x", (1,
    5)), ("h", (1, 1)), ("g", 4), ("h", (1, 2)), ("g", 5), ("h", (1, 3)), ("r", 4), ("r", 5), ("B", 0), ("A",
    1), ("s", 1), ("g", 6), ("d", (1, 0)), ("d", (1, 1)), ("c", 2), ("h", (2, 0)), ("h", (2, 1)), ("h", (2,
    2)), ("h", (2, 3)), ("f", 2), ("s", 2), ("f", 3), ("r", 6), ("d", (2, 0)), ("g", 7), ("B", 1), ("A", 2),
    ("d", (2, 1)), ("r", 7), ("B", 2), ("c", 3), ("f", 4), ("h", (3, 0)), ("A", 3), ("A", 4), ("f", 5), ("h",
    (3, 1)), ("B", 3), ("h", (3, 2)), ("h", (3, 3)), ("s", 3), ("d", (3, 0)), ("d", (3, 1)), ("B", 4), ("A",
    5), ("f", 6), ("A", 6), ("f", 7), ("B", 5), ("B", 6), ("A", 7), ("B", 7),
)


def plan(count, together, tiles):
    if (count, together, tiles) == (8, 2, 4):
        return EIGHT_ORDER, EIGHT_STEPS
    chips, groups = count // CORES, count // together
    order = [(j, p) for p in range(CORES) for j in range(chips)]
    steps = [("V", 0), ("q", 0)] + [("a", (0, i)) for i in range(PARTS)] + [("t", 0), ("m", 0), ("q", 1)]
    steps += [("a", (1, i)) for i in range(PARTS)] + [("m", 1)]
    steps += [("x", (p, k)) for p in range(CORES) for k in range(1, count)]
    ahead = together + 1
    gathered, passed = 0, 0

    def gather_to(last):
        nonlocal gathered, passed
        found = []
        while gathered <= min(last, count - 1):
            found.append(("g", gathered))
            gathered += 1
            if gathered > 1:
                found.append(("r", passed))
                passed += 1
        if last >= count and passed < count:
            found.append(("r", passed))
            passed += 1
        return found

    steps += gather_to(ahead)
    for p in range(groups):
        base = p * together
        steps.append(("c", p))
        for n in range(tiles):
            steps.append(("h", (p, n)))
            steps += gather_to(base + ahead + ((n + 1) * together + tiles - 1) // tiles)
        steps.append(("s", p))
        for part in range(2):
            steps.append(("d", (p, part)))
            for k in range(part * together // 2, (part + 1) * together // 2):
                if base > 0:
                    steps.append(("A", base - together + k))
                if base - together + k > 0:
                    steps.append(("B", base - together + k - 1))
        steps += [("f", base + i) for i in range(together)]
    for k in range((groups - 1) * together, count):
        steps += [("A", k), ("B", k - 1)]
    return order, steps + [("B", count - 1)]


def layer_kernel(
    seq_count, exp_count, tail, together, tile, wide_tile, norm_tile,
    pairs_ref, ids_ref, gate_weight_ref, gain_ref, in_hbm, q_hbm, k_hbm, v_hbm, gate_hbm, up_hbm, down_hbm,
    out_ref,
    present, x_in, q_run, k_run, v_run, attended, outgoing, got, choose_ref, coarse_ref, fine_ref,
    gate_ref, up_ref, down_ref, buf, x_ref, hid_ref, in0, in1, out0, out1, mid0, mid1, done,
    in_sem, own_sem, q_send, q_recv, f_send, f_recv, a_own, a_send, a_recv,
    local_sem, stay_sem, w_sem, z_send, z_recv, x_send, x_recv, d_send, d_recv,
    p_send, p_recv, m_send, m_recv, g_send, g_recv,
):
    s, e = lax.axis_index("seq"), lax.axis_index("exp")
    z, c = lax.div(e, CORES), lax.rem(e, CORES)
    chips = exp_count // CORES
    rows, width = x_in.shape
    run, group = q_run.shape
    heads, blocks, owners = group // HSZ, run // BLK, BLK // rows
    slots = DIST + 1
    capacity = buf.shape[3]
    inner_count = seq_count // OUTER
    half = width // 2
    a, b = lax.div(s, inner_count), lax.rem(s, inner_count)
    other = 1 - a
    outer = (other * inner_count + b, e)
    steps = range(1, inner_count)
    forth = [turned(b, j, inner_count) for j in steps]
    back = [turned(b, -j, inner_count) for j in steps]
    inner = [(a * inner_count + f, e) for f in forth]
    low, high = pl.ds(0, half), pl.ds(half, half)
    groups = exp_count // together
    chunk_rows = seq_count * capacity

    def arrived(block, send_sem, recv_sem):
        remote(block, block, send_sem, recv_sem, (s, e)).wait_recv()

    def columns(ref, index):
        return ref.at[:, pl.ds(pl.multiple_of(index * group, group), group)]

    def place(index):
        return lax.rem(index, CORES) * chips + lax.div(index, CORES)

    def lines(ref, offset, index):
        return ref.at[pl.ds(pl.multiple_of(offset + index * rows, rows), rows)]

    def landing(i, owner):
        if i == 2:
            return lines(q_run, 0, place(owner))
        return lines((k_run, v_run)[i], tail, owner)

    sources = (k_hbm, v_hbm, q_hbm)

    def give(i, k):
        d = xor(e, k, exp_count)
        return remote(columns(sources[i], d), landing(i, e), q_send.at[i, k], q_recv.at[i, k], (s, d))

    def keep(i):
        return pltpu.make_async_copy(columns(sources[i], e), landing(i, e), own_sem.at[i])

    def taken(i, k):
        block = landing(i, xor(e, k, exp_count))
        arrived(block, q_send.at[i, k], q_recv.at[i, k])

    def relay(i, k, act):
        owner = xor(e, k, exp_count)
        inside = (owner + 1) * rows > run - tail
        row = pl.multiple_of(lax.max(owner * rows - (run - tail), 0), rows)
        copy = remote(
            landing(i, owner), (k_run, v_run)[i].at[pl.ds(row, rows)], f_send.at[i, k], f_recv.at[i, k],
            (turned(s, 1, seq_count), e),
        )
        if act == "start":
            pl.when(inside & (s < seq_count - 1))(copy.start)
        elif act == "send":
            pl.when(inside & (s < seq_count - 1))(copy.wait_send)
        else:
            pl.when(inside & (s > 0))(copy.wait_recv)

    barrier = pltpu.get_barrier_semaphore()
    for k in range(1, exp_count):
        pl.semaphore_signal(barrier, inc=1, device_id=(s, turned(e, k, exp_count)), device_id_type=MESH)
    for k in range(1, seq_count):
        pl.semaphore_signal(barrier, inc=1, device_id=(turned(s, k, seq_count), e), device_id_type=MESH)
    pl.semaphore_wait(barrier, exp_count + seq_count - 2)

    for i in range(2):
        for k in range(1, exp_count):
            give(i, k).start()

    @pl.when(c == 0)
    def _():
        for k in range(1, exp_count):
            give(2, k).start()

    for i in range(3):
        keep(i).start()
    inputs_copy = pltpu.make_async_copy(in_hbm, x_in, in_sem)
    inputs_copy.start()
    weights = [
        pltpu.make_async_copy(source.at[0], target, w_sem.at[i])
        for i, (source, target) in enumerate(
            ((gate_hbm, gate_ref), (up_hbm, up_ref), (down_hbm, down_ref))
        )
    ]
    for copy in weights:
        copy.start()

    first_block = s * blocks
    wanted = [(first_block + i, first_block + i - (DIST - j)) for i in range(blocks) for j in range(slots)]

    def seen(p, found):
        query, key = pairs_ref[0, p], pairs_ref[1, p]
        return tuple(
            f + jnp.where((query == w[0]) & (key == w[1]), 1, 0) for f, w in zip(found, wanted)
        )

    found = lax.fori_loop(0, pairs_ref.shape[1], seen, (jnp.int32(0),) * len(wanted))
    for i in range(blocks):
        for j in range(slots):
            present[i, j] = found[i * slots + j]

    places = exp_count * capacity
    named = [ids_ref[t : t + 1, :] for t in range(TOP)]
    ranks = lax.broadcasted_iota(jnp.int32, (HSZ, rows), 0)
    marks = [jnp.where(n == ranks, 1.0, 0.0) for n in named]
    earlier = jnp.where(
        lax.broadcasted_iota(jnp.int32, (rows, rows), 0) < lax.broadcasted_iota(jnp.int32, (rows, rows), 1),
        1.0, 0.0,
    ).astype(jnp.bfloat16)
    ahead = jnp.dot(sum(marks).astype(jnp.bfloat16), earlier, preferred_element_type=jnp.float32)
    slot_ids = lax.broadcasted_iota(jnp.int32, (places, rows), 0)
    choose = jnp.zeros((places, rows), jnp.float32)
    weight = jnp.zeros((places, rows), jnp.float32)
    for t in range(TOP):
        position = jnp.sum(ahead * marks[t], axis=0, keepdims=True)
        spot = named[t] * capacity + position.astype(jnp.int32) == slot_ids
        choose = jnp.where(spot, 1.0, choose)
        weight = jnp.where(spot, gate_weight_ref[t : t + 1, :], weight)
    choose_ref[...] = choose.astype(jnp.bfloat16)
    weight = weight.T
    coarse = weight.astype(jnp.bfloat16)
    coarse_ref[...] = coarse
    fine_ref[...] = (weight - coarse.astype(jnp.float32)).astype(jnp.bfloat16)


    def queries_of(parity):
        for j in range(chips):
            k = CORES * j + lax.rem(c + parity, CORES)
            if j == 0:
                pl.when(k > 0)(functools.partial(taken, 2, k))
            else:
                taken(2, k)

    def late_queries():
        @pl.when(c > 0)
        def _():
            for k in range(1, exp_count):
                give(2, k).start()

    def keys_and_values():
        for i in range(2):
            keep(i).wait()
            relay(i, 0, "start")
            for k in range(1, exp_count):
                taken(i, k)
                relay(i, k, "start")
        keep(2).wait()
        for i in range(2):
            for k in range(exp_count):
                relay(i, k, "recv")

    scale = 1.0 / math.sqrt(HSZ)

    def piece(owner, head):
        return q_run.at[
            pl.ds(pl.multiple_of(place(owner) * rows, rows), rows), pl.ds(pl.multiple_of(head * HSZ, HSZ), HSZ)
        ]

    def goal(giver, head):
        return attended.at[:, pl.ds(pl.multiple_of(giver * group + head * HSZ, HSZ), HSZ)]

    def send(owner, head):
        return remote(
            piece(owner, head), goal(e, head), a_send.at[owner, head], a_recv.at[e, head], (s, owner)
        )

    def own(head):
        return pltpu.make_async_copy(piece(e, head), goal(e, head), a_own.at[head])

    part = BLK // CORES

    def attend(parity, begin, end):
        def step(i):
            head = lax.rem(i, heads)
            block = lax.rem(lax.div(e, owners) + 1 + lax.div(i, heads), blocks)
            column = pl.ds(pl.multiple_of(head * HSZ, HSZ), HSZ)
            mine = pl.ds(pl.multiple_of(parity * (run // CORES) + block * part, part), part)

            def span(slot):
                return pl.ds(pl.multiple_of((block + slot) * BLK, BLK), BLK)

            q = q_run[mine, column]
            scores = []
            for j in range(slots):
                score = lax.dot_general(
                    q, k_run[span(j), column], (((1,), (1,)), ((), ())), preferred_element_type=jnp.float32
                )
                scores.append(jnp.where(present[block, j] > 0, score * scale, very_negative))
            top = functools.reduce(jnp.maximum, [jnp.max(x, axis=1, keepdims=True) for x in scores])
            total, summed = 0.0, 0.0
            for j in range(slots):
                exps = jnp.exp(scores[j] - top)
                total = total + jnp.sum(exps, axis=1, keepdims=True)
                value = v_run[span(j), column]
                value = jnp.where(present[block, j] > 0, value, jnp.zeros_like(value))
                summed = summed + jnp.dot(
                    exps.astype(jnp.bfloat16), value, preferred_element_type=jnp.float32
                )
            q_run[mine, column] = (summed / total).astype(q_run.dtype)
            for j in range(owners // CORES):
                owner = block * owners + CORES * j + parity

                @pl.when(owner != e)
                def _():
                    send(owner, head).start()

                @pl.when(owner == e)
                def _():
                    own(head).start()

        loop(begin, end, step)

    def mixed(where):
        return wide(x_in[:, where]) + wide(attended[:, where])

    order, program = plan(exp_count, together, hid_ref.shape[1] // tile)

    def apart(k):
        j, p = order[k]
        return CORES * j + lax.rem(c + p, CORES)

    def chunk(k):
        j, p = order[k]
        return CORES * xor(z, j, chips) + p

    def here(k, act):
        j, p = order[k]
        if j == 0:
            pl.when(c == p)(act)

    def away(k, act):
        j, p = order[k]
        if j == 0:
            pl.when(c != p)(act)
        else:
            act()

    def spread(k):
        d = xor(e, k, exp_count)
        return remote(outgoing.at[d], buf.at[a, b, e], z_send.at[k], z_recv.at[k], (s, d))

    def stays():
        return pltpu.make_async_copy(outgoing.at[e], buf.at[a, b, e], local_sem)

    def dispatch():
        inputs_copy.wait()

        def squares(k, total):
            giver = xor(e, k, exp_count)

            @pl.when(k > 0)
            def _():
                for head in range(heads):
                    block = goal(giver, head)
                    arrived(block, a_send.at[giver, head], a_recv.at[giver, head])

            @pl.when(k == 0)
            def _():
                for head in range(heads):
                    own(head).wait()

            value = mixed(pl.ds(pl.multiple_of(giver * group, group), group))
            return total + jnp.sum(value * value, axis=1, keepdims=True)

        total = lax.fori_loop(0, exp_count, squares, jnp.zeros((rows, 1), jnp.float32))
        factor = lax.rsqrt(total / width + norm_epsilon)

        def normed_tile(n):
            where = pl.ds(pl.multiple_of(n * norm_tile, norm_tile), norm_tile)
            normed = (mixed(where) * factor * gain_ref[:, where]).astype(jnp.bfloat16)
            picked = jnp.dot(choose_ref[...], normed, preferred_element_type=jnp.float32)
            outgoing[:, :, where] = picked.astype(outgoing.dtype).reshape(exp_count, capacity, norm_tile)

        loop(0, width // norm_tile, normed_tile)
        stays().start()


    def directs(k):
        block = buf.at[a, b, chunk(k)]
        return [
            remote(block, block, x_send.at[i, k], x_recv.at[i, k], peer)
            for i, peer in enumerate([outer] + inner)
        ]

    def relays(k):
        n = chunk(k)
        copies = []
        for j, peer in enumerate(inner):
            block = buf.at[other, b, n, :, low]
            copies.append(remote(block, block, d_send.at[0, j, k], d_recv.at[0, j, k], peer))
            block = buf.at[a, back[j], n, :, high]
            copies.append(remote(block, block, d_send.at[1, j, k], d_recv.at[1, j, k], outer))
        return copies

    def gather(k):
        away(k, lambda: arrived(buf.at[a, b, chunk(k)], z_send.at[apart(k)], z_recv.at[apart(k)]))
        here(k, lambda: stays().wait())
        for copy in directs(k):
            copy.start()

    def pass_on(k):
        m = chunk(k)
        arrived(buf.at[other, b, m], x_send.at[0, k], x_recv.at[0, k])
        for j in range(inner_count - 1):
            arrived(buf.at[a, back[j], m], x_send.at[1 + j, k], x_recv.at[1 + j, k])
        for copy in relays(k):
            copy.start()

    def complete(k):
        n = chunk(k)
        for j in range(inner_count - 1):
            for h, side in enumerate((low, high)):
                arrived(buf.at[other, back[j], n, :, side], d_send.at[h, j, k], d_recv.at[h, j, k])

    def first(k):
        n = chunk(k)
        return [
            remote(buf.at[other, :, n, :, high], in1.at[k], p_send.at[0, k], p_recv.at[0, k], outer)
        ] + [
            remote(
                buf.at[:, f, n, :, low], in0.at[j, k], p_send.at[1 + j, k], p_recv.at[1 + j, k], inner[j]
            )
            for j, f in enumerate(forth)
        ]

    def second(k):
        return [remote(out0.at[k], mid0.at[k], m_send.at[0, k], m_recv.at[0, k], outer)] + [
            remote(out1.at[j, k], mid1.at[j, k], m_send.at[1 + j, k], m_recv.at[1 + j, k], inner[j])
            for j in range(inner_count - 1)
        ]

    def third(k):
        return remote(done.at[k], got.at[e], g_send.at[k], g_recv.at[apart(k)], (s, chunk(k)))

    def stay(k):
        return pltpu.make_async_copy(done.at[k], got.at[e], stay_sem)

    def inner_sum(k, side):
        total = wide(buf[side, b, chunk(k), :, low])
        for j in range(inner_count - 1):
            total = total + wide(in0[j, k, side])
        return total

    def outer_sum(k, lane):
        return wide(buf[a, lane, chunk(k), :, high]) + wide(in1[k, lane])

    def half_sum(k):
        sends = second(k)
        for j in range(inner_count - 1):
            arrived(in0.at[j, k], p_send.at[1 + j, k], p_recv.at[1 + j, k])
        out0[k] = inner_sum(k, other).astype(out0.dtype)
        sends[0].start()
        arrived(in1.at[k], p_send.at[0, k], p_recv.at[0, k])
        for j, f in enumerate(forth):
            out1[j, k] = outer_sum(k, f).astype(out1.dtype)
            sends[1 + j].start()

    def whole_sum(k):
        arrived(mid0.at[k], m_send.at[0, k], m_recv.at[0, k])
        done[k, :, low] = (inner_sum(k, a) + wide(mid0[k])).astype(done.dtype)
        total = outer_sum(k, b)
        for j in range(inner_count - 1):
            arrived(mid1.at[j, k], m_send.at[1 + j, k], m_recv.at[1 + j, k])
            total = total + wide(mid1[j, k])
        done[k, :, high] = total.astype(done.dtype)
        here(k, lambda: stay(k).start())
        away(k, lambda: third(k).start())

    tiles, wide_tiles = hid_ref.shape[1] // tile, width // wide_tile

    def collect(p):
        for i in range(together):
            k = p * together + i
            complete(k)
            x_ref[pl.ds(i * chunk_rows, chunk_rows)] = buf[:, :, chunk(k)].reshape(chunk_rows, width)

    def hidden_tile(n):
        where = pl.ds(n * tile, tile)
        x = x_ref[...]
        gate = jnp.dot(x, gate_ref[:, where], preferred_element_type=jnp.float32)
        up = jnp.dot(x, up_ref[:, where], preferred_element_type=jnp.float32)
        hid_ref[:, where] = (jax.nn.silu(gate) * up).astype(hid_ref.dtype)

    def gone(p):
        for i in range(together):
            for copy in directs(p * together + i) + relays(p * together + i):
                copy.wait_send()

    def down_tiles(p, begin, end):
        def down_tile(n):
            where = pl.ds(pl.multiple_of(n * wide_tile, wide_tile), wide_tile)
            y = jnp.dot(hid_ref[...], down_ref[:, where], preferred_element_type=jnp.float32).astype(buf.dtype)
            for i in range(together):
                buf[:, :, chunk(p * together + i), :, where] = y[
                    i * chunk_rows : (i + 1) * chunk_rows
                ].reshape(OUTER, inner_count, capacity, wide_tile)

        loop(begin, end, down_tile)

    def leave(k):
        for copy in first(k):
            copy.start()

    items = blocks * heads
    acts = {
        "V": lambda k: keys_and_values(),
        "q": queries_of,
        "t": lambda k: late_queries(),
        "a": lambda k: attend(k[0], k[1] * items // PARTS, (k[1] + 1) * items // PARTS),
        "m": lambda k: pl.when(c == k)(dispatch),
        "x": lambda k: pl.when(c == k[0])(lambda: spread(k[1]).start()),
        "g": gather,
        "r": pass_on,
        "c": collect,
        "h": lambda k: hidden_tile(k[1]),
        "s": gone,
        "d": lambda k: down_tiles(k[0], k[1] * wide_tiles // 2, (k[1] + 1) * wide_tiles // 2),
        "f": leave,
        "A": half_sum,
        "B": whole_sum,
    }
    for name, k in program:
        if name == "c" and k == 0:
            for copy in weights:
                copy.wait()
        acts[name](k)

    for k in range(exp_count):
        here(k, lambda: stay(k).wait())
    for k in range(1, exp_count):
        arrived(got.at[xor(e, k, exp_count)], g_send.at[k], g_recv.at[k])

    def final_tile(n):
        where = pl.ds(pl.multiple_of(n * norm_tile, norm_tile), norm_tile)
        flat = got[:, :, where].reshape(places, norm_tile)
        combined = jnp.dot(coarse_ref[...], flat, preferred_element_type=jnp.float32) + jnp.dot(
            fine_ref[...], flat, preferred_element_type=jnp.float32
        )
        out_ref[:, where] = (mixed(where) + combined).astype(out_ref.dtype)

    loop(0, width // norm_tile, final_tile)

    for i in range(2):
        for k in range(exp_count):
            relay(i, k, "send")
    for i in range(3):
        for k in range(1, exp_count):
            give(i, k).wait_send()

    for k in range(exp_count):
        for copy in first(k) + second(k):
            copy.wait_send()
        away(k, lambda: third(k).wait_send())

    def finish(k):
        spread(k).wait_send()
        for head in range(heads):
            send(xor(e, k, exp_count), head).wait_send()

    loop(1, exp_count, finish)


def per_device(
    inputs, queries, keys, values, norm_gain, expert_ids, gate_weights, pairs, w_gate, w_up, w_down
):
    rows, width = inputs.shape
    seq_count, exp_count = lax.axis_size("seq"), lax.axis_size("exp")
    tail = DIST * BLK
    run, group = rows * exp_count, queries.shape[1] // exp_count
    heads, blocks = group // HSZ, run // BLK
    capacity = rows * TOP // exp_count
    places = exp_count * capacity
    hidden = w_gate.shape[2]
    inner_count = seq_count // OUTER
    inner_peers = inner_count - 1
    half = width // 2
    kind = inputs.dtype
    together = 1
    while 2 * together * seq_count * capacity <= 256 and exp_count % (2 * together) == 0:
        together *= 2
    group_rows = together * seq_count * capacity
    tile, wide_tile, norm_tile = min(256, hidden // together), min(512, width // together), min(512, width)
    vmem = [
        (rows, width),
        (run, group),
        (tail + run, group),
        (tail + run, group),
        (rows, width),
        (exp_count, capacity, width),
        (exp_count, capacity, width),
        (places, rows),
        (rows, places),
        (rows, places),
        w_gate.shape[1:],
        w_up.shape[1:],
        w_down.shape[1:],
        (OUTER, inner_count, exp_count, capacity, width),
        (group_rows, width),
        (group_rows, hidden),
        (inner_peers, exp_count, OUTER, capacity, half),
        (exp_count, inner_count, capacity, half),
        (exp_count, capacity, half),
        (inner_peers, exp_count, capacity, half),
        (exp_count, capacity, half),
        (inner_peers, exp_count, capacity, half),
        (exp_count, capacity, width),
    ]
    one, per_peer, per_side = (exp_count,), (inner_count, exp_count), (2, inner_peers, exp_count)
    sems = [
        (3, exp_count), (3, exp_count), (2, exp_count), (2, exp_count), (heads,), (exp_count, heads),
        (exp_count, heads),
    ]
    more = [one, one, per_peer, per_peer, per_side, per_side, per_peer, per_peer, per_peer, per_peer, one, one]
    return pl.pallas_call(
        functools.partial(layer_kernel, seq_count, exp_count, tail, together, tile, wide_tile, norm_tile),
        out_shape=jax.ShapeDtypeStruct((rows, width), kind),
        in_specs=[pl.BlockSpec(memory_space=pltpu.SMEM)] + [HELD] * 3 + [ANY] * 7,
        out_specs=HELD,
        scratch_shapes=[pltpu.SMEM((blocks, DIST + 1), jnp.int32)]
        + [pltpu.VMEM(shape, kind) for shape in vmem]
        + [DMA, DMA((3,))]
        + [DMA(shape) for shape in sems]
        + [DMA, DMA, DMA((3,))]
        + [DMA(shape) for shape in more],
        compiler_params=pltpu.CompilerParams(
            collective_id=1, has_side_effects=True, vmem_limit_bytes=67043328
        ),
        name="layer",
    )(
        pairs.T, expert_ids.T, gate_weights.T, norm_gain.reshape(1, width), inputs, queries, keys, values,
        w_gate, w_up, w_down,
    )


def solution(mesh):
    rows = P(("seq", "exp"), None)
    in_specs = (
        rows, rows, rows, rows, P(), rows, rows, P(),
        P("exp", None, "seq"), P("exp", None, "seq"), P("exp", "seq", None),
    )
    return jax.shard_map(
        per_device, mesh=mesh, in_specs=in_specs, out_specs=rows, check_vma=False
    )
```

```python
import functools
import math

import jax
import jax.numpy as jnp
from jax import lax
from jax.experimental import pallas as pl
from jax.experimental.pallas import tpu as pltpu
from jax.sharding import PartitionSpec as P

HSZ = 128
TOP = 2
BLK = 512
DIST = 2
OUTER = 2
CORES = 2
PARTS = 4

very_negative = -1e30
norm_epsilon = 1e-05

MESH = pl.DeviceIdType.MESH
ANY = pl.BlockSpec(memory_space=pl.ANY)
HELD = pl.BlockSpec(memory_space=pltpu.VMEM)
DMA = pltpu.SemaphoreType.DMA


def remote(source, target, send_sem, recv_sem, device):
    return pltpu.make_async_remote_copy(
        src_ref=source,
        dst_ref=target,
        send_sem=send_sem,
        recv_sem=recv_sem,
        device_id=device,
        device_id_type=MESH,
    )


def turned(index, steps, count):
    return lax.rem(index + (steps % count), count)


def xor(one, two, count):
    total, bit = 0, 1
    while bit < count:
        total = total + bit * lax.rem(lax.div(one, bit) + lax.div(two, bit), 2)
        bit *= 2
    return total


def loop(begin, end, body):
    def step(i, carry):
        body(i)
        return carry

    lax.fori_loop(begin, end, step, 0)


def wide(value):
    return value.astype(jnp.float32)


EIGHT_ORDER = ((0, 0), (1, 0), (3, 0), (2, 0), (3, 1), (2, 1), (1, 1), (0, 1))
EIGHT_STEPS = (
    ("V", 0), ("q", 0), ("a", (0, 0)), ("a", (0, 1)), ("a", (0, 2)), ("a", (0, 3)), ("m", 0), ("x", (0, 1)),
    ("x", (0, 2)), ("t", 0), ("x", (0, 3)), ("x", (0, 6)), ("x", (0, 7)), ("x", (0, 4)), ("x", (0, 5)), ("g",
    0), ("g", 1), ("r", 0), ("r", 1), ("c", 0), ("q", 1), ("h", (0, 0)), ("h", (0, 1)), ("g", 2), ("h", (0,
    2)), ("h", (0, 3)), ("g", 3), ("a", (1, 0)), ("r", 2), ("s", 0), ("a", (1, 1)), ("d", (0, 0)), ("r", 3),
    ("a", (1, 2)), ("d", (0, 1)), ("f", 0), ("f", 1), ("a", (1, 3)), ("c", 1), ("h", (1, 0)), ("A", 0), ("m",
    1), ("x", (1, 6)), ("h", (1, 1)), ("x", (1, 1)), ("h", (1, 2)), ("h", (1, 3)), ("x", (1, 7)), ("A", 1),
    ("s", 1), ("d", (1, 0)), ("x", (1, 2)), ("d", (1, 1)), ("x", (1, 5)), ("x", (1, 4)), ("f", 2), ("B", 0),
    ("f", 3), ("A", 2), ("x", (1, 3)), ("g", 4), ("B", 1), ("g", 5), ("r", 4), ("r", 5), ("g", 6), ("c", 2),
    ("B", 2), ("g", 7), ("h", (2, 0)), ("h", (2, 1)), ("h", (2, 2)), ("r", 6), ("h", (2, 3)), ("s", 2), ("r",
    7), ("d", (2, 0)), ("d", (2, 1)), ("A", 3), ("f", 4), ("c", 3), ("B", 3), ("h", (3, 0)), ("h", (3, 1)),
    ("A", 4), ("f", 5), ("h", (3, 2)), ("h", (3, 3)), ("B", 4), ("s", 3), ("d", (3, 0)), ("d", (3, 1)), ("f",
    6), ("A", 5), ("A", 6), ("f", 7), ("B", 5), ("B", 6), ("A", 7), ("B", 7),
)


def plan(count, together, tiles):
    if (count, together, tiles) == (8, 2, 4):
        return EIGHT_ORDER, EIGHT_STEPS
    chips, groups = count // CORES, count // together
    order = [(j, p) for p in range(CORES) for j in range(chips)]
    steps = [("V", 0), ("q", 0)] + [("a", (0, i)) for i in range(PARTS)] + [("t", 0), ("m", 0), ("q", 1)]
    steps += [("a", (1, i)) for i in range(PARTS)] + [("m", 1)]
    steps += [("x", (p, k)) for p in range(CORES) for k in range(1, count)]
    ahead = together + 1
    gathered, passed = 0, 0

    def gather_to(last):
        nonlocal gathered, passed
        found = []
        while gathered <= min(last, count - 1):
            found.append(("g", gathered))
            gathered += 1
            if gathered > 1:
                found.append(("r", passed))
                passed += 1
        if last >= count and passed < count:
            found.append(("r", passed))
            passed += 1
        return found

    steps += gather_to(ahead)
    for p in range(groups):
        base = p * together
        steps.append(("c", p))
        for n in range(tiles):
            steps.append(("h", (p, n)))
            steps += gather_to(base + ahead + ((n + 1) * together + tiles - 1) // tiles)
        steps.append(("s", p))
        for part in range(2):
            steps.append(("d", (p, part)))
            for k in range(part * together // 2, (part + 1) * together // 2):
                if base > 0:
                    steps.append(("A", base - together + k))
                if base - together + k > 0:
                    steps.append(("B", base - together + k - 1))
        steps += [("f", base + i) for i in range(together)]
    for k in range((groups - 1) * together, count):
        steps += [("A", k), ("B", k - 1)]
    return order, steps + [("B", count - 1)]


def layer_kernel(
    seq_count, exp_count, tail, together, tile, wide_tile, norm_tile,
    pairs_ref, ids_ref, gate_weight_ref, gain_ref, in_hbm, q_hbm, k_hbm, v_hbm, gate_hbm, up_hbm, down_hbm,
    out_ref,
    present, x_in, q_run, k_run, v_run, attended, outgoing, got, choose_ref, coarse_ref, fine_ref,
    gate_ref, up_ref, down_ref, buf, x_ref, hid_ref, in0, in1, out0, out1, mid0, mid1, done,
    in_sem, own_sem, q_send, q_recv, f_send, f_recv, a_own, a_send, a_recv,
    local_sem, stay_sem, w_sem, z_send, z_recv, x_send, x_recv, d_send, d_recv,
    p_send, p_recv, m_send, m_recv, g_send, g_recv,
):
    s, e = lax.axis_index("seq"), lax.axis_index("exp")
    z, c = lax.div(e, CORES), lax.rem(e, CORES)
    chips = exp_count // CORES
    rows, width = x_in.shape
    run, group = q_run.shape
    heads, blocks, owners = group // HSZ, run // BLK, BLK // rows
    slots = DIST + 1
    capacity = buf.shape[3]
    inner_count = seq_count // OUTER
    half = width // 2
    a, b = lax.div(s, inner_count), lax.rem(s, inner_count)
    other = 1 - a
    outer = (other * inner_count + b, e)
    steps = range(1, inner_count)
    forth = [turned(b, j, inner_count) for j in steps]
    back = [turned(b, -j, inner_count) for j in steps]
    inner = [(a * inner_count + f, e) for f in forth]
    low, high = pl.ds(0, half), pl.ds(half, half)
    groups = exp_count // together
    chunk_rows = seq_count * capacity

    def arrived(block, send_sem, recv_sem):
        remote(block, block, send_sem, recv_sem, (s, e)).wait_recv()

    def columns(ref, index):
        return ref.at[:, pl.ds(pl.multiple_of(index * group, group), group)]

    def place(index):
        return lax.rem(index, CORES) * chips + lax.div(index, CORES)

    def lines(ref, offset, index):
        return ref.at[pl.ds(pl.multiple_of(offset + index * rows, rows), rows)]

    def landing(i, owner):
        if i == 2:
            return lines(q_run, 0, place(owner))
        return lines((k_run, v_run)[i], tail, owner)

    sources = (k_hbm, v_hbm, q_hbm)

    def give(i, k):
        d = xor(e, k, exp_count)
        return remote(columns(sources[i], d), landing(i, e), q_send.at[i, k], q_recv.at[i, k], (s, d))

    def keep(i):
        return pltpu.make_async_copy(columns(sources[i], e), landing(i, e), own_sem.at[i])

    def taken(i, k):
        block = landing(i, xor(e, k, exp_count))
        arrived(block, q_send.at[i, k], q_recv.at[i, k])

    def relay(i, k, act):
        owner = xor(e, k, exp_count)
        inside = (owner + 1) * rows > run - tail
        row = pl.multiple_of(lax.max(owner * rows - (run - tail), 0), rows)
        copy = remote(
            landing(i, owner), (k_run, v_run)[i].at[pl.ds(row, rows)], f_send.at[i, k], f_recv.at[i, k],
            (turned(s, 1, seq_count), e),
        )
        if act == "start":
            pl.when(inside & (s < seq_count - 1))(copy.start)
        elif act == "send":
            pl.when(inside & (s < seq_count - 1))(copy.wait_send)
        else:
            pl.when(inside & (s > 0))(copy.wait_recv)

    barrier = pltpu.get_barrier_semaphore()
    for k in range(1, exp_count):
        pl.semaphore_signal(barrier, inc=1, device_id=(s, turned(e, k, exp_count)), device_id_type=MESH)
    for k in range(1, seq_count):
        pl.semaphore_signal(barrier, inc=1, device_id=(turned(s, k, seq_count), e), device_id_type=MESH)
    pl.semaphore_wait(barrier, exp_count + seq_count - 2)

    for i in range(2):
        for k in range(1, exp_count):
            give(i, k).start()

    @pl.when(c == 0)
    def _():
        for k in range(1, exp_count):
            give(2, k).start()

    for i in range(3):
        keep(i).start()
    inputs_copy = pltpu.make_async_copy(in_hbm, x_in, in_sem)
    inputs_copy.start()
    weights = [
        pltpu.make_async_copy(source.at[0], target, w_sem.at[i])
        for i, (source, target) in enumerate(
            ((gate_hbm, gate_ref), (up_hbm, up_ref), (down_hbm, down_ref))
        )
    ]
    for copy in weights:
        copy.start()

    first_block = s * blocks
    wanted = [(first_block + i, first_block + i - (DIST - j)) for i in range(blocks) for j in range(slots)]

    def seen(p, found):
        query, key = pairs_ref[0, p], pairs_ref[1, p]
        return tuple(
            f + jnp.where((query == w[0]) & (key == w[1]), 1, 0) for f, w in zip(found, wanted)
        )

    found = lax.fori_loop(0, pairs_ref.shape[1], seen, (jnp.int32(0),) * len(wanted))
    for i in range(blocks):
        for j in range(slots):
            present[i, j] = found[i * slots + j]

    places = exp_count * capacity
    named = [ids_ref[t : t + 1, :] for t in range(TOP)]
    ranks = lax.broadcasted_iota(jnp.int32, (HSZ, rows), 0)
    marks = [jnp.where(n == ranks, 1.0, 0.0) for n in named]
    earlier = jnp.where(
        lax.broadcasted_iota(jnp.int32, (rows, rows), 0) < lax.broadcasted_iota(jnp.int32, (rows, rows), 1),
        1.0, 0.0,
    ).astype(jnp.bfloat16)
    ahead = jnp.dot(sum(marks).astype(jnp.bfloat16), earlier, preferred_element_type=jnp.float32)
    slot_ids = lax.broadcasted_iota(jnp.int32, (places, rows), 0)
    choose = jnp.zeros((places, rows), jnp.float32)
    weight = jnp.zeros((places, rows), jnp.float32)
    for t in range(TOP):
        position = jnp.sum(ahead * marks[t], axis=0, keepdims=True)
        spot = named[t] * capacity + position.astype(jnp.int32) == slot_ids
        choose = jnp.where(spot, 1.0, choose)
        weight = jnp.where(spot, gate_weight_ref[t : t + 1, :], weight)
    choose_ref[...] = choose.astype(jnp.bfloat16)
    weight = weight.T
    coarse = weight.astype(jnp.bfloat16)
    coarse_ref[...] = coarse
    fine_ref[...] = (weight - coarse.astype(jnp.float32)).astype(jnp.bfloat16)


    def queries_of(parity):
        for j in range(chips):
            k = CORES * j + lax.rem(c + parity, CORES)
            if j == 0:
                pl.when(k > 0)(functools.partial(taken, 2, k))
            else:
                taken(2, k)

    def late_queries():
        @pl.when(c > 0)
        def _():
            for k in range(1, exp_count):
                give(2, k).start()

    def keys_and_values():
        for i in range(2):
            keep(i).wait()
            relay(i, 0, "start")
            for k in range(1, exp_count):
                taken(i, k)
                relay(i, k, "start")
        keep(2).wait()
        for i in range(2):
            for k in range(exp_count):
                relay(i, k, "recv")

    scale = 1.0 / math.sqrt(HSZ)

    def piece(owner, head):
        return q_run.at[
            pl.ds(pl.multiple_of(place(owner) * rows, rows), rows), pl.ds(pl.multiple_of(head * HSZ, HSZ), HSZ)
        ]

    def goal(giver, head):
        return attended.at[:, pl.ds(pl.multiple_of(giver * group + head * HSZ, HSZ), HSZ)]

    def send(owner, head):
        return remote(
            piece(owner, head), goal(e, head), a_send.at[owner, head], a_recv.at[e, head], (s, owner)
        )

    def own(head):
        return pltpu.make_async_copy(piece(e, head), goal(e, head), a_own.at[head])

    part = BLK // CORES

    def attend(parity, begin, end):
        def step(i):
            head = lax.rem(i, heads)
            block = lax.rem(lax.div(e, owners) + 1 + lax.div(i, heads), blocks)
            column = pl.ds(pl.multiple_of(head * HSZ, HSZ), HSZ)
            mine = pl.ds(pl.multiple_of(parity * (run // CORES) + block * part, part), part)

            def span(slot):
                return pl.ds(pl.multiple_of((block + slot) * BLK, BLK), BLK)

            q = q_run[mine, column]
            scores = []
            for j in range(slots):
                score = lax.dot_general(
                    q, k_run[span(j), column], (((1,), (1,)), ((), ())), preferred_element_type=jnp.float32
                )
                scores.append(jnp.where(present[block, j] > 0, score * scale, very_negative))
            top = functools.reduce(jnp.maximum, [jnp.max(x, axis=1, keepdims=True) for x in scores])
            total, summed = 0.0, 0.0
            for j in range(slots):
                exps = jnp.exp(scores[j] - top)
                total = total + jnp.sum(exps, axis=1, keepdims=True)
                value = v_run[span(j), column]
                value = jnp.where(present[block, j] > 0, value, jnp.zeros_like(value))
                summed = summed + jnp.dot(
                    exps.astype(jnp.bfloat16), value, preferred_element_type=jnp.float32
                )
            q_run[mine, column] = (summed / total).astype(q_run.dtype)
            for j in range(owners // CORES):
                owner = block * owners + CORES * j + parity

                @pl.when(owner != e)
                def _():
                    send(owner, head).start()

                @pl.when(owner == e)
                def _():
                    own(head).start()

        loop(begin, end, step)

    def mixed(where):
        return wide(x_in[:, where]) + wide(attended[:, where])

    order, program = plan(exp_count, together, hid_ref.shape[1] // tile)

    def apart(k):
        j, p = order[k]
        return CORES * j + lax.rem(c + p, CORES)

    def chunk(k):
        j, p = order[k]
        return CORES * xor(z, j, chips) + p

    def here(k, act):
        j, p = order[k]
        if j == 0:
            pl.when(c == p)(act)

    def away(k, act):
        j, p = order[k]
        if j == 0:
            pl.when(c != p)(act)
        else:
            act()

    def spread(k):
        d = xor(e, k, exp_count)
        return remote(outgoing.at[d], buf.at[a, b, e], z_send.at[k], z_recv.at[k], (s, d))

    def stays():
        return pltpu.make_async_copy(outgoing.at[e], buf.at[a, b, e], local_sem)

    def dispatch():
        inputs_copy.wait()

        def squares(k, total):
            giver = xor(e, k, exp_count)

            @pl.when(k > 0)
            def _():
                for head in range(heads):
                    block = goal(giver, head)
                    arrived(block, a_send.at[giver, head], a_recv.at[giver, head])

            @pl.when(k == 0)
            def _():
                for head in range(heads):
                    own(head).wait()

            value = mixed(pl.ds(pl.multiple_of(giver * group, group), group))
            return total + jnp.sum(value * value, axis=1, keepdims=True)

        total = lax.fori_loop(0, exp_count, squares, jnp.zeros((rows, 1), jnp.float32))
        factor = lax.rsqrt(total / width + norm_epsilon)

        def normed_tile(n):
            where = pl.ds(pl.multiple_of(n * norm_tile, norm_tile), norm_tile)
            normed = (mixed(where) * factor * gain_ref[:, where]).astype(jnp.bfloat16)
            picked = jnp.dot(choose_ref[...], normed, preferred_element_type=jnp.float32)
            outgoing[:, :, where] = picked.astype(outgoing.dtype).reshape(exp_count, capacity, norm_tile)

        loop(0, width // norm_tile, normed_tile)
        stays().start()


    def directs(k):
        block = buf.at[a, b, chunk(k)]
        return [
            remote(block, block, x_send.at[i, k], x_recv.at[i, k], peer)
            for i, peer in enumerate([outer] + inner)
        ]

    def relays(k):
        n = chunk(k)
        copies = []
        for j, peer in enumerate(inner):
            block = buf.at[other, b, n, :, low]
            copies.append(remote(block, block, d_send.at[0, j, k], d_recv.at[0, j, k], peer))
            block = buf.at[a, back[j], n, :, high]
            copies.append(remote(block, block, d_send.at[1, j, k], d_recv.at[1, j, k], outer))
        return copies

    def gather(k):
        away(k, lambda: arrived(buf.at[a, b, chunk(k)], z_send.at[apart(k)], z_recv.at[apart(k)]))
        here(k, lambda: stays().wait())
        for copy in directs(k):
            copy.start()

    def pass_on(k):
        m = chunk(k)
        arrived(buf.at[other, b, m], x_send.at[0, k], x_recv.at[0, k])
        for j in range(inner_count - 1):
            arrived(buf.at[a, back[j], m], x_send.at[1 + j, k], x_recv.at[1 + j, k])
        for copy in relays(k):
            copy.start()

    def complete(k):
        n = chunk(k)
        for j in range(inner_count - 1):
            for h, side in enumerate((low, high)):
                arrived(buf.at[other, back[j], n, :, side], d_send.at[h, j, k], d_recv.at[h, j, k])

    def first(k):
        n = chunk(k)
        return [
            remote(buf.at[other, :, n, :, high], in1.at[k], p_send.at[0, k], p_recv.at[0, k], outer)
        ] + [
            remote(
                buf.at[:, f, n, :, low], in0.at[j, k], p_send.at[1 + j, k], p_recv.at[1 + j, k], inner[j]
            )
            for j, f in enumerate(forth)
        ]

    def second(k):
        return [remote(out0.at[k], mid0.at[k], m_send.at[0, k], m_recv.at[0, k], outer)] + [
            remote(out1.at[j, k], mid1.at[j, k], m_send.at[1 + j, k], m_recv.at[1 + j, k], inner[j])
            for j in range(inner_count - 1)
        ]

    def third(k):
        return remote(done.at[k], got.at[e], g_send.at[k], g_recv.at[apart(k)], (s, chunk(k)))

    def stay(k):
        return pltpu.make_async_copy(done.at[k], got.at[e], stay_sem)

    def inner_sum(k, side):
        total = wide(buf[side, b, chunk(k), :, low])
        for j in range(inner_count - 1):
            total = total + wide(in0[j, k, side])
        return total

    def outer_sum(k, lane):
        return wide(buf[a, lane, chunk(k), :, high]) + wide(in1[k, lane])

    def half_sum(k):
        sends = second(k)
        for j in range(inner_count - 1):
            arrived(in0.at[j, k], p_send.at[1 + j, k], p_recv.at[1 + j, k])
        out0[k] = inner_sum(k, other).astype(out0.dtype)
        sends[0].start()
        arrived(in1.at[k], p_send.at[0, k], p_recv.at[0, k])
        for j, f in enumerate(forth):
            out1[j, k] = outer_sum(k, f).astype(out1.dtype)
            sends[1 + j].start()

    def whole_sum(k):
        arrived(mid0.at[k], m_send.at[0, k], m_recv.at[0, k])
        done[k, :, low] = (inner_sum(k, a) + wide(mid0[k])).astype(done.dtype)
        total = outer_sum(k, b)
        for j in range(inner_count - 1):
            arrived(mid1.at[j, k], m_send.at[1 + j, k], m_recv.at[1 + j, k])
            total = total + wide(mid1[j, k])
        done[k, :, high] = total.astype(done.dtype)
        here(k, lambda: stay(k).start())
        away(k, lambda: third(k).start())

    tiles, wide_tiles = hid_ref.shape[1] // tile, width // wide_tile

    def collect(p):
        for i in range(together):
            k = p * together + i
            complete(k)
            x_ref[pl.ds(i * chunk_rows, chunk_rows)] = buf[:, :, chunk(k)].reshape(chunk_rows, width)

    def hidden_tile(n):
        where = pl.ds(n * tile, tile)
        x = x_ref[...]
        gate = jnp.dot(x, gate_ref[:, where], preferred_element_type=jnp.float32)
        up = jnp.dot(x, up_ref[:, where], preferred_element_type=jnp.float32)
        hid_ref[:, where] = (jax.nn.silu(gate) * up).astype(hid_ref.dtype)

    def gone(p):
        for i in range(together):
            for copy in directs(p * together + i) + relays(p * together + i):
                copy.wait_send()

    def down_tiles(p, begin, end):
        def down_tile(n):
            where = pl.ds(pl.multiple_of(n * wide_tile, wide_tile), wide_tile)
            y = jnp.dot(hid_ref[...], down_ref[:, where], preferred_element_type=jnp.float32).astype(buf.dtype)
            for i in range(together):
                buf[:, :, chunk(p * together + i), :, where] = y[
                    i * chunk_rows : (i + 1) * chunk_rows
                ].reshape(OUTER, inner_count, capacity, wide_tile)

        loop(begin, end, down_tile)

    def leave(k):
        for copy in first(k):
            copy.start()

    items = blocks * heads
    acts = {
        "V": lambda k: keys_and_values(),
        "q": queries_of,
        "t": lambda k: late_queries(),
        "a": lambda k: attend(k[0], k[1] * items // PARTS, (k[1] + 1) * items // PARTS),
        "m": lambda k: pl.when(c == k)(dispatch),
        "x": lambda k: pl.when(c == k[0])(lambda: spread(k[1]).start()),
        "g": gather,
        "r": pass_on,
        "c": collect,
        "h": lambda k: hidden_tile(k[1]),
        "s": gone,
        "d": lambda k: down_tiles(k[0], k[1] * wide_tiles // 2, (k[1] + 1) * wide_tiles // 2),
        "f": leave,
        "A": half_sum,
        "B": whole_sum,
    }
    for name, k in program:
        if name == "c" and k == 0:
            for copy in weights:
                copy.wait()
        acts[name](k)

    for k in range(exp_count):
        here(k, lambda: stay(k).wait())
    for k in range(1, exp_count):
        arrived(got.at[xor(e, k, exp_count)], g_send.at[k], g_recv.at[k])

    def final_tile(n):
        where = pl.ds(pl.multiple_of(n * norm_tile, norm_tile), norm_tile)
        flat = got[:, :, where].reshape(places, norm_tile)
        combined = jnp.dot(coarse_ref[...], flat, preferred_element_type=jnp.float32) + jnp.dot(
            fine_ref[...], flat, preferred_element_type=jnp.float32
        )
        out_ref[:, where] = (mixed(where) + combined).astype(out_ref.dtype)

    loop(0, width // norm_tile, final_tile)

    for i in range(2):
        for k in range(exp_count):
            relay(i, k, "send")
    for i in range(3):
        for k in range(1, exp_count):
            give(i, k).wait_send()

    for k in range(exp_count):
        for copy in first(k) + second(k):
            copy.wait_send()
        away(k, lambda: third(k).wait_send())

    def finish(k):
        spread(k).wait_send()
        for head in range(heads):
            send(xor(e, k, exp_count), head).wait_send()

    loop(1, exp_count, finish)


def per_device(
    inputs, queries, keys, values, norm_gain, expert_ids, gate_weights, pairs, w_gate, w_up, w_down
):
    rows, width = inputs.shape
    seq_count, exp_count = lax.axis_size("seq"), lax.axis_size("exp")
    tail = DIST * BLK
    run, group = rows * exp_count, queries.shape[1] // exp_count
    heads, blocks = group // HSZ, run // BLK
    capacity = rows * TOP // exp_count
    places = exp_count * capacity
    hidden = w_gate.shape[2]
    inner_count = seq_count // OUTER
    inner_peers = inner_count - 1
    half = width // 2
    kind = inputs.dtype
    together = 1
    while 2 * together * seq_count * capacity <= 256 and exp_count % (2 * together) == 0:
        together *= 2
    group_rows = together * seq_count * capacity
    tile, wide_tile, norm_tile = min(256, hidden // together), min(512, width // together), min(512, width)
    vmem = [
        (rows, width),
        (run, group),
        (tail + run, group),
        (tail + run, group),
        (rows, width),
        (exp_count, capacity, width),
        (exp_count, capacity, width),
        (places, rows),
        (rows, places),
        (rows, places),
        w_gate.shape[1:],
        w_up.shape[1:],
        w_down.shape[1:],
        (OUTER, inner_count, exp_count, capacity, width),
        (group_rows, width),
        (group_rows, hidden),
        (inner_peers, exp_count, OUTER, capacity, half),
        (exp_count, inner_count, capacity, half),
        (exp_count, capacity, half),
        (inner_peers, exp_count, capacity, half),
        (exp_count, capacity, half),
        (inner_peers, exp_count, capacity, half),
        (exp_count, capacity, width),
    ]
    one, per_peer, per_side = (exp_count,), (inner_count, exp_count), (2, inner_peers, exp_count)
    sems = [
        (3, exp_count), (3, exp_count), (2, exp_count), (2, exp_count), (heads,), (exp_count, heads),
        (exp_count, heads),
    ]
    more = [one, one, per_peer, per_peer, per_side, per_side, per_peer, per_peer, per_peer, per_peer, one, one]
    return pl.pallas_call(
        functools.partial(layer_kernel, seq_count, exp_count, tail, together, tile, wide_tile, norm_tile),
        out_shape=jax.ShapeDtypeStruct((rows, width), kind),
        in_specs=[pl.BlockSpec(memory_space=pltpu.SMEM)] + [HELD] * 3 + [ANY] * 7,
        out_specs=HELD,
        scratch_shapes=[pltpu.SMEM((blocks, DIST + 1), jnp.int32)]
        + [pltpu.VMEM(shape, kind) for shape in vmem]
        + [DMA, DMA((3,))]
        + [DMA(shape) for shape in sems]
        + [DMA, DMA, DMA((3,))]
        + [DMA(shape) for shape in more],
        compiler_params=pltpu.CompilerParams(
            collective_id=1, has_side_effects=True, vmem_limit_bytes=67043328
        ),
        name="layer",
    )(
        pairs.T, expert_ids.T, gate_weights.T, norm_gain.reshape(1, width), inputs, queries, keys, values,
        w_gate, w_up, w_down,
    )


def solution(mesh):
    rows = P(("seq", "exp"), None)
    in_specs = (
        rows, rows, rows, rows, P(), rows, rows, P(),
        P("exp", None, "seq"), P("exp", None, "seq"), P("exp", "seq", None),
    )
    return jax.shard_map(
        per_device, mesh=mesh, in_specs=in_specs, out_specs=rows, check_vma=False
    )
```

```python
import functools
import math

import jax
import jax.numpy as jnp
from jax import lax
from jax.experimental import pallas as pl
from jax.experimental.pallas import tpu as pltpu
from jax.sharding import PartitionSpec as P

HSZ = 128
TOP = 2
BLK = 512
DIST = 2
OUTER = 2
CORES = 2
PARTS = 4

very_negative = -1e30
norm_epsilon = 1e-05

MESH = pl.DeviceIdType.MESH
ANY = pl.BlockSpec(memory_space=pl.ANY)
HELD = pl.BlockSpec(memory_space=pltpu.VMEM)
DMA = pltpu.SemaphoreType.DMA


def remote(source, target, send_sem, recv_sem, device):
    return pltpu.make_async_remote_copy(
        src_ref=source,
        dst_ref=target,
        send_sem=send_sem,
        recv_sem=recv_sem,
        device_id=device,
        device_id_type=MESH,
    )


def turned(index, steps, count):
    return lax.rem(index + (steps % count), count)


def xor(one, two, count):
    total, bit = 0, 1
    while bit < count:
        total = total + bit * lax.rem(lax.div(one, bit) + lax.div(two, bit), 2)
        bit *= 2
    return total


def loop(begin, end, body):
    def step(i, carry):
        body(i)
        return carry

    lax.fori_loop(begin, end, step, 0)


def wide(value):
    return value.astype(jnp.float32)


EIGHT_ORDER = ((0, 0), (1, 0), (3, 0), (2, 0), (3, 1), (2, 1), (1, 1), (0, 1))
EIGHT_STEPS = (
    ("V", 0), ("q", 0), ("a", (0, 0)), ("a", (0, 1)), ("a", (0, 2)), ("a", (0, 3)), ("m", 0), ("t", 0), ("x",
    (0, 2)), ("x", (0, 3)), ("x", (0, 6)), ("x", (0, 1)), ("x", (0, 7)), ("x", (0, 4)), ("x", (0, 5)), ("g",
    0), ("g", 1), ("R", 0), ("r", 0), ("r", 1), ("R", 1), ("c", 0), ("q", 1), ("h", (0, 0)), ("h", (0, 1)),
    ("g", 2), ("h", (0, 2)), ("h", (0, 3)), ("s", 0), ("g", 3), ("d", (0, 0)), ("a", (1, 0)), ("d", (0, 1)),
    ("r", 2), ("R", 2), ("R", 3), ("r", 3), ("F", 0), ("f", 0), ("F", 1), ("a", (1, 1)), ("a", (1, 2)), ("a",
    (1, 3)), ("c", 1), ("f", 1), ("h", (1, 0)), ("A", 0), ("h", (1, 1)), ("E", 0), ("h", (1, 2)), ("m", 1),
    ("x", (1, 7)), ("x", (1, 1)), ("h", (1, 3)), ("x", (1, 6)), ("x", (1, 3)), ("s", 1), ("d", (1, 0)), ("x",
    (1, 5)), ("f", 2), ("A", 1), ("x", (1, 4)), ("d", (1, 1)), ("F", 2), ("E", 1), ("f", 3), ("B", 0), ("F",
    3), ("E", 2), ("x", (1, 2)), ("A", 2), ("g", 4), ("R", 4), ("g", 5), ("B", 1), ("g", 6), ("r", 4), ("R",
    5), ("B", 2), ("r", 5), ("c", 2), ("g", 7), ("E", 3), ("R", 6), ("A", 3), ("h", (2, 0)), ("h", (2, 1)),
    ("r", 6), ("h", (2, 2)), ("R", 7), ("r", 7), ("h", (2, 3)), ("s", 2), ("d", (2, 0)), ("f", 4), ("d", (2,
    1)), ("F", 4), ("B", 3), ("c", 3), ("h", (3, 0)), ("h", (3, 1)), ("E", 4), ("f", 5), ("A", 4), ("h", (3,
    2)), ("F", 5), ("h", (3, 3)), ("s", 3), ("B", 4), ("d", (3, 0)), ("d", (3, 1)), ("f", 6), ("F", 6), ("A",
    5), ("E", 5), ("E", 6), ("A", 6), ("B", 5), ("f", 7), ("F", 7), ("B", 6), ("A", 7), ("E", 7), ("B", 7),
)


def plan(count, together, tiles):
    if (count, together, tiles) == (8, 2, 4):
        return EIGHT_ORDER, EIGHT_STEPS
    chips, groups = count // CORES, count // together
    order = [(j, p) for p in range(CORES) for j in range(chips)]
    steps = [("V", 0), ("q", 0)] + [("a", (0, i)) for i in range(PARTS)] + [("t", 0), ("m", 0), ("q", 1)]
    steps += [("a", (1, i)) for i in range(PARTS)] + [("m", 1)]
    steps += [("x", (p, k)) for p in range(CORES) for k in range(1, count)]
    ahead = together + 1
    gathered, passed = 0, 0

    def gather_to(last):
        nonlocal gathered, passed
        found = []
        while gathered <= min(last, count - 1):
            found.append(("g", gathered))
            gathered += 1
            if gathered > 1:
                found.append(("r", passed))
                passed += 1
        if last >= count and passed < count:
            found.append(("r", passed))
            passed += 1
        return found

    steps += gather_to(ahead)
    for p in range(groups):
        base = p * together
        steps.append(("c", p))
        for n in range(tiles):
            steps.append(("h", (p, n)))
            steps += gather_to(base + ahead + ((n + 1) * together + tiles - 1) // tiles)
        steps.append(("s", p))
        for part in range(2):
            steps.append(("d", (p, part)))
            for k in range(part * together // 2, (part + 1) * together // 2):
                if base > 0:
                    steps.append(("A", base - together + k))
                if base - together + k > 0:
                    steps.append(("B", base - together + k - 1))
        steps += [("f", base + i) for i in range(together)]
    for k in range((groups - 1) * together, count):
        steps += [("A", k), ("B", k - 1)]
    steps += [("B", count - 1)]
    pairs = {"r": "rR", "f": "Ff", "A": "AE"}
    return order, [(name, k) for step, k in steps for name in pairs.get(step, step)]


def layer_kernel(
    seq_count, exp_count, tail, together, tile, wide_tile, norm_tile,
    pairs_ref, ids_ref, gate_weight_ref, gain_ref, in_hbm, q_hbm, k_hbm, v_hbm, gate_hbm, up_hbm, down_hbm,
    out_ref,
    present, x_in, q_run, k_run, v_run, attended, outgoing, got, choose_ref, coarse_ref, fine_ref,
    gate_ref, up_ref, down_ref, buf, x_ref, hid_ref, in0, in1, out0, out1, mid0, mid1, done,
    in_sem, own_sem, q_send, q_recv, f_send, f_recv, a_own, a_send, a_recv,
    local_sem, stay_sem, w_sem, z_send, z_recv, x_send, x_recv, d_send, d_recv,
    p_send, p_recv, m_send, m_recv, g_send, g_recv, put_sem,
):
    s, e = lax.axis_index("seq"), lax.axis_index("exp")
    z, c = lax.div(e, CORES), lax.rem(e, CORES)
    chips = exp_count // CORES
    rows, width = x_in.shape
    run, group = q_run.shape
    heads, blocks, owners = group // HSZ, run // BLK, BLK // rows
    slots = DIST + 1
    capacity = buf.shape[3]
    inner_count = seq_count // OUTER
    half = width // 2
    a, b = lax.div(s, inner_count), lax.rem(s, inner_count)
    other = 1 - a
    outer = (other * inner_count + b, e)
    steps = range(1, inner_count)
    forth = [turned(b, j, inner_count) for j in steps]
    back = [turned(b, -j, inner_count) for j in steps]
    inner = [(a * inner_count + f, e) for f in forth]
    low, high = pl.ds(0, half), pl.ds(half, half)
    groups = exp_count // together
    chunk_rows = seq_count * capacity

    def arrived(block, send_sem, recv_sem):
        remote(block, block, send_sem, recv_sem, (s, e)).wait_recv()

    def columns(ref, index):
        return ref.at[:, pl.ds(pl.multiple_of(index * group, group), group)]

    def place(index):
        return lax.rem(index, CORES) * chips + lax.div(index, CORES)

    def lines(ref, offset, index):
        return ref.at[pl.ds(pl.multiple_of(offset + index * rows, rows), rows)]

    def landing(i, owner):
        if i == 2:
            return lines(q_run, 0, place(owner))
        return lines((k_run, v_run)[i], tail, owner)

    sources = (k_hbm, v_hbm, q_hbm)

    def give(i, k):
        d = xor(e, k, exp_count)
        return remote(columns(sources[i], d), landing(i, e), q_send.at[i, k], q_recv.at[i, k], (s, d))

    def keep(i):
        return pltpu.make_async_copy(columns(sources[i], e), landing(i, e), own_sem.at[i])

    def taken(i, k):
        block = landing(i, xor(e, k, exp_count))
        arrived(block, q_send.at[i, k], q_recv.at[i, k])

    def relay(i, k, act):
        owner = xor(e, k, exp_count)
        inside = (owner + 1) * rows > run - tail
        row = pl.multiple_of(lax.max(owner * rows - (run - tail), 0), rows)
        copy = remote(
            landing(i, owner), (k_run, v_run)[i].at[pl.ds(row, rows)], f_send.at[i, k], f_recv.at[i, k],
            (turned(s, 1, seq_count), e),
        )
        if act == "start":
            pl.when(inside & (s < seq_count - 1))(copy.start)
        elif act == "send":
            pl.when(inside & (s < seq_count - 1))(copy.wait_send)
        else:
            pl.when(inside & (s > 0))(copy.wait_recv)

    barrier = pltpu.get_barrier_semaphore()
    for k in range(1, exp_count):
        pl.semaphore_signal(barrier, inc=1, device_id=(s, turned(e, k, exp_count)), device_id_type=MESH)
    for k in range(1, seq_count):
        pl.semaphore_signal(barrier, inc=1, device_id=(turned(s, k, seq_count), e), device_id_type=MESH)
    pl.semaphore_wait(barrier, exp_count + seq_count - 2)

    for i in range(2):
        for k in range(1, exp_count):
            give(i, k).start()

    @pl.when(c == 0)
    def _():
        for k in range(1, exp_count):
            give(2, k).start()

    for i in range(3):
        keep(i).start()
    inputs_copy = pltpu.make_async_copy(in_hbm, x_in, in_sem)
    inputs_copy.start()
    weights = [
        pltpu.make_async_copy(source.at[0], target, w_sem.at[i])
        for i, (source, target) in enumerate(
            ((gate_hbm, gate_ref), (up_hbm, up_ref), (down_hbm, down_ref))
        )
    ]
    for copy in weights:
        copy.start()

    first_block = s * blocks
    wanted = [(first_block + i, first_block + i - (DIST - j)) for i in range(blocks) for j in range(slots)]

    def seen(p, found):
        query, key = pairs_ref[0, p], pairs_ref[1, p]
        return tuple(
            f + jnp.where((query == w[0]) & (key == w[1]), 1, 0) for f, w in zip(found, wanted)
        )

    found = lax.fori_loop(0, pairs_ref.shape[1], seen, (jnp.int32(0),) * len(wanted))
    for i in range(blocks):
        for j in range(slots):
            present[i, j] = found[i * slots + j]

    places = exp_count * capacity
    named = [ids_ref[t : t + 1, :] for t in range(TOP)]
    ranks = lax.broadcasted_iota(jnp.int32, (HSZ, rows), 0)
    marks = [jnp.where(n == ranks, 1.0, 0.0) for n in named]
    earlier = jnp.where(
        lax.broadcasted_iota(jnp.int32, (rows, rows), 0) < lax.broadcasted_iota(jnp.int32, (rows, rows), 1),
        1.0, 0.0,
    ).astype(jnp.bfloat16)
    ahead = jnp.dot(sum(marks).astype(jnp.bfloat16), earlier, preferred_element_type=jnp.float32)
    slot_ids = lax.broadcasted_iota(jnp.int32, (places, rows), 0)
    choose = jnp.zeros((places, rows), jnp.float32)
    weight = jnp.zeros((places, rows), jnp.float32)
    for t in range(TOP):
        position = jnp.sum(ahead * marks[t], axis=0, keepdims=True)
        spot = named[t] * capacity + position.astype(jnp.int32) == slot_ids
        choose = jnp.where(spot, 1.0, choose)
        weight = jnp.where(spot, gate_weight_ref[t : t + 1, :], weight)
    choose_ref[...] = choose.astype(jnp.bfloat16)
    weight = weight.T
    coarse = weight.astype(jnp.bfloat16)
    coarse_ref[...] = coarse
    fine_ref[...] = (weight - coarse.astype(jnp.float32)).astype(jnp.bfloat16)


    def queries_of(parity):
        for j in range(chips):
            k = CORES * j + lax.rem(c + parity, CORES)
            if j == 0:
                pl.when(k > 0)(functools.partial(taken, 2, k))
            else:
                taken(2, k)

    def late_queries():
        @pl.when(c > 0)
        def _():
            for k in range(1, exp_count):
                give(2, k).start()

    def keys_and_values():
        for i in range(2):
            keep(i).wait()
            relay(i, 0, "start")
            for k in range(1, exp_count):
                taken(i, k)
                relay(i, k, "start")
        keep(2).wait()
        for i in range(2):
            for k in range(exp_count):
                relay(i, k, "recv")

    scale = 1.0 / math.sqrt(HSZ)

    def piece(owner, head):
        return q_run.at[
            pl.ds(pl.multiple_of(place(owner) * rows, rows), rows), pl.ds(pl.multiple_of(head * HSZ, HSZ), HSZ)
        ]

    def goal(giver, head):
        return attended.at[:, pl.ds(pl.multiple_of(giver * group + head * HSZ, HSZ), HSZ)]

    def send(owner, head):
        return remote(
            piece(owner, head), goal(e, head), a_send.at[owner, head], a_recv.at[e, head], (s, owner)
        )

    def own(head):
        return pltpu.make_async_copy(piece(e, head), goal(e, head), a_own.at[head])

    part = BLK // CORES

    def attend(parity, begin, end):
        def step(i):
            head = lax.rem(i, heads)
            block = lax.rem(lax.div(e, owners) + 1 + lax.div(i, heads), blocks)
            column = pl.ds(pl.multiple_of(head * HSZ, HSZ), HSZ)
            mine = pl.ds(pl.multiple_of(parity * (run // CORES) + block * part, part), part)

            def span(slot):
                return pl.ds(pl.multiple_of((block + slot) * BLK, BLK), BLK)

            q = q_run[mine, column]
            scores = []
            for j in range(slots):
                score = lax.dot_general(
                    q, k_run[span(j), column], (((1,), (1,)), ((), ())), preferred_element_type=jnp.float32
                )
                scores.append(jnp.where(present[block, j] > 0, score * scale, very_negative))
            top = functools.reduce(jnp.maximum, [jnp.max(x, axis=1, keepdims=True) for x in scores])
            total, summed = 0.0, 0.0
            for j in range(slots):
                exps = jnp.exp(scores[j] - top)
                total = total + jnp.sum(exps, axis=1, keepdims=True)
                value = v_run[span(j), column]
                value = jnp.where(present[block, j] > 0, value, jnp.zeros_like(value))
                summed = summed + jnp.dot(
                    exps.astype(jnp.bfloat16), value, preferred_element_type=jnp.float32
                )
            q_run[mine, column] = (summed / total).astype(q_run.dtype)
            for j in range(owners // CORES):
                owner = block * owners + CORES * j + parity

                @pl.when(owner != e)
                def _():
                    send(owner, head).start()

                @pl.when(owner == e)
                def _():
                    own(head).start()

        loop(begin, end, step)

    def mixed(where):
        return wide(x_in[:, where]) + wide(attended[:, where])

    order, program = plan(exp_count, together, hid_ref.shape[1] // tile)

    def apart(k):
        j, p = order[k]
        return CORES * j + lax.rem(c + p, CORES)

    def chunk(k):
        j, p = order[k]
        return CORES * xor(z, j, chips) + p

    def here(k, act):
        j, p = order[k]
        if j == 0:
            pl.when(c == p)(act)

    def away(k, act):
        j, p = order[k]
        if j == 0:
            pl.when(c != p)(act)
        else:
            act()

    def spread(k):
        d = xor(e, k, exp_count)
        return remote(outgoing.at[d], buf.at[a, b, e], z_send.at[k], z_recv.at[k], (s, d))

    def stays():
        return pltpu.make_async_copy(outgoing.at[e], buf.at[a, b, e], local_sem)

    def dispatch():
        inputs_copy.wait()

        def squares(k, total):
            giver = xor(e, k, exp_count)

            @pl.when(k > 0)
            def _():
                for head in range(heads):
                    block = goal(giver, head)
                    arrived(block, a_send.at[giver, head], a_recv.at[giver, head])

            @pl.when(k == 0)
            def _():
                for head in range(heads):
                    own(head).wait()

            value = mixed(pl.ds(pl.multiple_of(giver * group, group), group))
            return total + jnp.sum(value * value, axis=1, keepdims=True)

        total = lax.fori_loop(0, exp_count, squares, jnp.zeros((rows, 1), jnp.float32))
        factor = lax.rsqrt(total / width + norm_epsilon)

        def normed_tile(n):
            where = pl.ds(pl.multiple_of(n * norm_tile, norm_tile), norm_tile)
            normed = (mixed(where) * factor * gain_ref[:, where]).astype(jnp.bfloat16)
            picked = jnp.dot(choose_ref[...], normed, preferred_element_type=jnp.float32)
            outgoing[:, :, where] = picked.astype(outgoing.dtype).reshape(exp_count, capacity, norm_tile)

        loop(0, width // norm_tile, normed_tile)
        stays().start()


    def directs(k):
        block = buf.at[a, b, chunk(k)]
        return [
            remote(block, block, x_send.at[i, k], x_recv.at[i, k], peer)
            for i, peer in enumerate([outer] + inner)
        ]

    def relays(k):
        n = chunk(k)
        copies = []
        for j, peer in enumerate(inner):
            block = buf.at[other, b, n, :, low]
            copies.append(remote(block, block, d_send.at[0, j, k], d_recv.at[0, j, k], peer))
            block = buf.at[a, back[j], n, :, high]
            copies.append(remote(block, block, d_send.at[1, j, k], d_recv.at[1, j, k], outer))
        return copies

    def gather(k):
        away(k, lambda: arrived(buf.at[a, b, chunk(k)], z_send.at[apart(k)], z_recv.at[apart(k)]))
        here(k, lambda: stays().wait())
        for copy in directs(k):
            copy.start()

    def pass_low(k):
        arrived(buf.at[other, b, chunk(k)], x_send.at[0, k], x_recv.at[0, k])
        for copy in relays(k)[0::2]:
            copy.start()

    def pass_high(k):
        for j in range(inner_count - 1):
            arrived(buf.at[a, back[j], chunk(k)], x_send.at[1 + j, k], x_recv.at[1 + j, k])
        for copy in relays(k)[1::2]:
            copy.start()

    def complete(k):
        n = chunk(k)
        for j in range(inner_count - 1):
            for h, side in enumerate((low, high)):
                arrived(buf.at[other, back[j], n, :, side], d_send.at[h, j, k], d_recv.at[h, j, k])

    def first(k):
        n = chunk(k)
        return [
            remote(buf.at[other, :, n, :, high], in1.at[k], p_send.at[0, k], p_recv.at[0, k], outer)
        ] + [
            remote(
                buf.at[:, f, n, :, low], in0.at[j, k], p_send.at[1 + j, k], p_recv.at[1 + j, k], inner[j]
            )
            for j, f in enumerate(forth)
        ]

    def second(k):
        return [remote(out0.at[k], mid0.at[k], m_send.at[0, k], m_recv.at[0, k], outer)] + [
            remote(out1.at[j, k], mid1.at[j, k], m_send.at[1 + j, k], m_recv.at[1 + j, k], inner[j])
            for j in range(inner_count - 1)
        ]

    def third(k):
        return remote(done.at[k], got.at[e], g_send.at[k], g_recv.at[apart(k)], (s, chunk(k)))

    def stay(k):
        return pltpu.make_async_copy(done.at[k], got.at[e], stay_sem)

    def inner_sum(k, side):
        total = wide(buf[side, b, chunk(k), :, low])
        for j in range(inner_count - 1):
            total = total + wide(in0[j, k, side])
        return total

    def outer_sum(k, lane):
        return wide(buf[a, lane, chunk(k), :, high]) + wide(in1[k, lane])

    def low_sum(k):
        for j in range(inner_count - 1):
            arrived(in0.at[j, k], p_send.at[1 + j, k], p_recv.at[1 + j, k])
        out0[k] = inner_sum(k, other).astype(out0.dtype)
        second(k)[0].start()

    def high_sum(k):
        arrived(in1.at[k], p_send.at[0, k], p_recv.at[0, k])
        for j, f in enumerate(forth):
            out1[j, k] = outer_sum(k, f).astype(out1.dtype)
            second(k)[1 + j].start()

    def whole_sum(k):
        arrived(mid0.at[k], m_send.at[0, k], m_recv.at[0, k])
        done[k, :, low] = (inner_sum(k, a) + wide(mid0[k])).astype(done.dtype)
        total = outer_sum(k, b)
        for j in range(inner_count - 1):
            arrived(mid1.at[j, k], m_send.at[1 + j, k], m_recv.at[1 + j, k])
            total = total + wide(mid1[j, k])
        done[k, :, high] = total.astype(done.dtype)
        here(k, lambda: stay(k).start())
        away(k, lambda: third(k).start())

    tiles, wide_tiles = hid_ref.shape[1] // tile, width // wide_tile

    def collect(p):
        for i in range(together):
            k = p * together + i
            complete(k)
            x_ref[pl.ds(i * chunk_rows, chunk_rows)] = buf[:, :, chunk(k)].reshape(chunk_rows, width)

    def hidden_tile(n):
        where = pl.ds(n * tile, tile)
        x = x_ref[...]
        gate = jnp.dot(x, gate_ref[:, where], preferred_element_type=jnp.float32)
        up = jnp.dot(x, up_ref[:, where], preferred_element_type=jnp.float32)
        hid_ref[:, where] = (jax.nn.silu(gate) * up).astype(hid_ref.dtype)

    def gone(p):
        for i in range(together):
            for copy in directs(p * together + i) + relays(p * together + i):
                copy.wait_send()

    def down_tiles(p, begin, end):
        def down_tile(n):
            where = pl.ds(pl.multiple_of(n * wide_tile, wide_tile), wide_tile)
            y = jnp.dot(hid_ref[...], down_ref[:, where], preferred_element_type=jnp.float32).astype(buf.dtype)
            for i in range(together):
                buf[:, :, chunk(p * together + i), :, where] = y[
                    i * chunk_rows : (i + 1) * chunk_rows
                ].reshape(OUTER, inner_count, capacity, wide_tile)

        loop(begin, end, down_tile)

    def leave_low(k):
        for copy in first(k)[1:]:
            copy.start()

    def leave_high(k):
        first(k)[0].start()

    items = blocks * heads
    acts = {
        "V": lambda k: keys_and_values(),
        "q": queries_of,
        "t": lambda k: late_queries(),
        "a": lambda k: attend(k[0], k[1] * items // PARTS, (k[1] + 1) * items // PARTS),
        "m": lambda k: pl.when(c == k)(dispatch),
        "x": lambda k: pl.when(c == k[0])(lambda: spread(k[1]).start()),
        "g": gather,
        "r": pass_low,
        "R": pass_high,
        "c": collect,
        "h": lambda k: hidden_tile(k[1]),
        "s": gone,
        "d": lambda k: down_tiles(k[0], k[1] * wide_tiles // 2, (k[1] + 1) * wide_tiles // 2),
        "f": leave_low,
        "F": leave_high,
        "A": low_sum,
        "E": high_sum,
        "B": whole_sum,
    }
    for name, k in program:
        if name == "c" and k == 0:
            for copy in weights:
                copy.wait()
        acts[name](k)

    for k in range(exp_count):
        here(k, lambda: stay(k).wait())
    for k in range(1, exp_count):
        arrived(got.at[xor(e, k, exp_count)], g_send.at[k], g_recv.at[k])

    def put(n):
        where = pl.ds(pl.multiple_of(n * norm_tile, norm_tile), norm_tile)
        return pltpu.make_async_copy(x_in.at[:, where], out_ref.at[:, where], put_sem.at[n])

    def final_tile(n):
        where = pl.ds(pl.multiple_of(n * norm_tile, norm_tile), norm_tile)
        flat = got[:, :, where].reshape(places, norm_tile)
        combined = jnp.dot(coarse_ref[...], flat, preferred_element_type=jnp.float32) + jnp.dot(
            fine_ref[...], flat, preferred_element_type=jnp.float32
        )
        x_in[:, where] = (mixed(where) + combined).astype(x_in.dtype)
        put(n).start()

    loop(0, width // norm_tile, final_tile)

    for i in range(2):
        for k in range(exp_count):
            relay(i, k, "send")
    for i in range(3):
        for k in range(1, exp_count):
            give(i, k).wait_send()

    for k in range(exp_count):
        for copy in first(k) + second(k):
            copy.wait_send()
        away(k, lambda: third(k).wait_send())

    def finish(k):
        spread(k).wait_send()
        for head in range(heads):
            send(xor(e, k, exp_count), head).wait_send()

    loop(1, exp_count, finish)
    loop(0, width // norm_tile, lambda n: put(n).wait())


def per_device(
    inputs, queries, keys, values, norm_gain, expert_ids, gate_weights, pairs, w_gate, w_up, w_down
):
    rows, width = inputs.shape
    seq_count, exp_count = lax.axis_size("seq"), lax.axis_size("exp")
    tail = DIST * BLK
    run, group = rows * exp_count, queries.shape[1] // exp_count
    heads, blocks = group // HSZ, run // BLK
    capacity = rows * TOP // exp_count
    places = exp_count * capacity
    hidden = w_gate.shape[2]
    inner_count = seq_count // OUTER
    inner_peers = inner_count - 1
    half = width // 2
    kind = inputs.dtype
    together = 1
    while 2 * together * seq_count * capacity <= 256 and exp_count % (2 * together) == 0:
        together *= 2
    group_rows = together * seq_count * capacity
    tile, wide_tile, norm_tile = min(256, hidden // together), min(512, width // together), min(512, width)
    vmem = [
        (rows, width),
        (run, group),
        (tail + run, group),
        (tail + run, group),
        (rows, width),
        (exp_count, capacity, width),
        (exp_count, capacity, width),
        (places, rows),
        (rows, places),
        (rows, places),
        w_gate.shape[1:],
        w_up.shape[1:],
        w_down.shape[1:],
        (OUTER, inner_count, exp_count, capacity, width),
        (group_rows, width),
        (group_rows, hidden),
        (inner_peers, exp_count, OUTER, capacity, half),
        (exp_count, inner_count, capacity, half),
        (exp_count, capacity, half),
        (inner_peers, exp_count, capacity, half),
        (exp_count, capacity, half),
        (inner_peers, exp_count, capacity, half),
        (exp_count, capacity, width),
    ]
    one, per_peer, per_side = (exp_count,), (inner_count, exp_count), (2, inner_peers, exp_count)
    sems = [
        (3, exp_count), (3, exp_count), (2, exp_count), (2, exp_count), (heads,), (exp_count, heads),
        (exp_count, heads),
    ]
    more = [one, one, per_peer, per_peer, per_side, per_side, per_peer, per_peer, per_peer, per_peer, one, one]
    return pl.pallas_call(
        functools.partial(layer_kernel, seq_count, exp_count, tail, together, tile, wide_tile, norm_tile),
        out_shape=jax.ShapeDtypeStruct((rows, width), kind),
        in_specs=[pl.BlockSpec(memory_space=pltpu.SMEM)] + [HELD] * 3 + [ANY] * 7,
        out_specs=ANY,
        scratch_shapes=[pltpu.SMEM((blocks, DIST + 1), jnp.int32)]
        + [pltpu.VMEM(shape, kind) for shape in vmem]
        + [DMA, DMA((3,))]
        + [DMA(shape) for shape in sems]
        + [DMA, DMA, DMA((3,))]
        + [DMA(shape) for shape in more]
        + [DMA((width // norm_tile,))],
        compiler_params=pltpu.CompilerParams(
            collective_id=1, has_side_effects=True, vmem_limit_bytes=67043328
        ),
        name="layer",
    )(
        pairs.T, expert_ids.T, gate_weights.T, norm_gain.reshape(1, width), inputs, queries, keys, values,
        w_gate, w_up, w_down,
    )


def solution(mesh):
    rows = P(("seq", "exp"), None)
    in_specs = (
        rows, rows, rows, rows, P(), rows, rows, P(),
        P("exp", None, "seq"), P("exp", None, "seq"), P("exp", "seq", None),
    )
    return jax.shard_map(
        per_device, mesh=mesh, in_specs=in_specs, out_specs=rows, check_vma=False
    )
```
